128 devices in a mesh: pts: 8 (over y, core), cen: 16 (over x, z).
Axes of the slice: x: 4, y: 4, z: 4, core: 2. Of those that a mesh axis runs over, the one named last changes fastest.
Arguments:
- points: bfloat16 [32768, 1024], P('pts'), may hold values from -128 to 128
- centroids: float32 [8192, 1024], P('cen'), may hold values from -10 to 10
Outputs:
- centroid_means: float32 [8192, 1024], P('cen', 'pts')
- log_norms: float32 [32768], P('pts')
The draws below stay inside these ranges and needn't reach their ends.
All inputs are finite; a program needn't handle non-finite values.
Results may differ from the reference program's by a relative error of at most 0.0015.
The reference program's roundings to bfloat16 on the way (of `unit_rows` and `weights`) count: a program that leaves them out, or rounds other values in their place, can miss the bound.
Values may be sent and summed in bfloat16 or wider, within the bound.
A program may use at most 64 MiB of HBM per device.

```python
import math
import jax
import jax.numpy as jnp
from jax import lax

D = 1024
K = 8192
ITERS = 2
PTS = 32768


def centroid_base(key):
    feature_key, value_key = jax.random.split(jax.random.fold_in(key, 11))
    feature_scale = jnp.exp(jax.random.uniform(feature_key, (1, D), jnp.float32, math.log(0.5), math.log(2.0)))
    values = jnp.clip(jax.random.normal(value_key, (K, D), jnp.float32), -5.0, 5.0)
    return values * feature_scale


def draw_centroids(key, part):
    return centroid_base(key)


def draw_points(key, part):
    row_key, value_key = jax.random.split(jax.random.fold_in(key, 23), 2)
    row_scale = jnp.exp(jax.random.uniform(row_key, (PTS, 1), jnp.float32, math.log(0.3), math.log(3.0)))
    result = jnp.clip(jax.random.normal(value_key, (PTS, D), jnp.float32), -5.0, 5.0) * row_scale
    return jnp.clip(result, -128.0, 128.0).astype(jnp.bfloat16)


def setup_inputs(seed: int = 0) -> dict:
    key_list = jax.random.split(jax.random.key(seed), 3)
    points = draw_points(jax.random.fold_in(key_list[2], 71), 0)
    centroids = draw_centroids(jax.random.fold_in(key_list[2], 71), 0)
    return {"points": points, "centroids": centroids}


def normalize_rows(rows):
    return rows * lax.rsqrt(lax.optimization_barrier(jnp.sum(rows * rows, axis=1, keepdims=True)) + 1e-06)

def reference(points, centroids):
    total_rows = points.shape[0]
    block_rows = min(total_rows, 1024)
    block_count = total_rows // block_rows
    blocks = points.reshape(block_count, block_rows, D)
    unit_rows = normalize_rows(centroids).astype(jnp.bfloat16)
    centroid_means = centroids
    log_values = jnp.zeros((block_count, block_rows), jnp.float32)
    for iteration in range(ITERS):
        current = unit_rows

        def visit(carry, block):
            weighted, point_mass = carry
            logits = jnp.dot(block, current.T, preferred_element_type=jnp.float32)
            row_max = lax.optimization_barrier(jnp.max(logits, axis=1))
            shifted = jnp.exp(logits - row_max[:, None])
            row_total = lax.optimization_barrier(jnp.sum(shifted, axis=1))
            weights = (shifted / row_total[:, None]).astype(jnp.bfloat16)
            weighted = weighted + jnp.dot(weights.T, block, preferred_element_type=jnp.float32)
            point_mass = point_mass + lax.optimization_barrier(jnp.sum(weights.astype(jnp.float32), axis=0))
            return ((weighted, point_mass), row_max + jnp.log(row_total))
        start = (jnp.zeros((K, D), jnp.float32), jnp.zeros((K,), jnp.float32))
        (weighted, point_mass), log_values = lax.scan(visit, start, blocks)
        centroid_means = weighted / jnp.maximum(point_mass, 1.0)[:, None]
        unit_rows = normalize_rows(centroid_means).astype(jnp.bfloat16)
    return (centroid_means, log_values.reshape(total_rows))
```

```python
import functools
import jax
import jax.numpy as jnp
from jax import lax
from jax.experimental import pallas as pl
from jax.experimental.pallas import tpu as pltpu
from jax.sharding import PartitionSpec as P

ITERS = 2
MESH = pl.DeviceIdType.MESH
F32 = jnp.float32
BF16 = jnp.bfloat16
CHUNK = 1024
COLS = 256


def kernel(
    pts_hbm, cen_hbm, means_out, log_out,
    pts, cen, unit, expd, wts, mass, max_loc, stat, acc, pair, sib_buf, y_buf, col_buf,
    mass_all, mass_col, sums,
    in_sem, st_send, st_recv, sib_send, sib_recv, y_send, y_recv, m_send, m_recv,
    g_send, g_recv, gs_send, gs_recv,
):
    p = lax.axis_index("pts")
    c = lax.axis_index("cen")
    y, core = p // 2, lax.rem(p, 2)
    other = 1 - core
    n_chunks = pts.shape[0] // CHUNK
    n_cols = pts.shape[1] // COLS

    def at_y(k):
        return lax.rem(y + k, 4)

    def y_peer(k):
        return (at_y(k) * 2 + core, c)

    sibling = (y * 2 + other, c)

    def load_points(i):
        rows = pl.ds(pl.multiple_of(i * CHUNK, CHUNK), CHUNK)
        return pltpu.make_async_copy(pts_hbm.at[rows], pts.at[rows], in_sem.at[i])

    load_cen = pltpu.make_async_copy(cen_hbm, cen, in_sem.at[n_chunks])
    load_cen.start()

    @pl.loop(0, n_chunks)
    def _(i):
        load_points(i).start()

    barrier = pltpu.get_barrier_semaphore()

    @pl.loop(1, 16)
    def _(i):
        pl.semaphore_signal(barrier, inc=1, device_id=(p, lax.rem(c + i, 16)), device_id_type=MESH)

    @pl.loop(1, 8)
    def _(i):
        pl.semaphore_signal(barrier, inc=1, device_id=(lax.rem(p + i, 8), c), device_id_type=MESH)

    load_cen.wait()

    @pl.loop(0, 8)
    def _(b):
        rows = pl.ds(pl.multiple_of(b * 64, 64), 64)
        v = cen[rows, :]
        squares = jnp.sum(v * v, axis=1, keepdims=True)
        unit[0, rows, :] = (v * lax.rsqrt(squares + 1e-06)).astype(BF16)

    pl.semaphore_wait(barrier, 22)

    def stat_copy(it, ch, i, slot):
        return pltpu.make_async_remote_copy(
            src_ref=stat.at[it, ch, c], dst_ref=stat.at[it, ch, slot],
            send_sem=st_send.at[it, ch, i], recv_sem=st_recv.at[it, ch, slot],
            device_id=(p, lax.rem(c + i, 16)), device_id_type=MESH,
        )

    def sib_copy(it, n):
        if it == 0:
            src = acc.at[it, n, pl.ds(pl.multiple_of(other * 256, 256), 256), :]
            dst = sib_buf.at[n]
        else:
            src = acc.at[it, n, :, pl.ds(pl.multiple_of(other * 128, 128), 128)]
            dst = col_buf.at[n]
        return pltpu.make_async_remote_copy(
            src_ref=src, dst_ref=dst, send_sem=sib_send.at[it, n], recv_sem=sib_recv.at[it, n],
            device_id=sibling, device_id_type=MESH,
        )

    def y_copy_rows(n, k):
        return pltpu.make_async_remote_copy(
            src_ref=pair.at[n, pl.ds(pl.multiple_of(at_y(k) * 64, 64), 64), :],
            dst_ref=y_buf.at[n, k - 1],
            send_sem=y_send.at[0, n, k - 1], recv_sem=y_recv.at[0, n, k - 1],
            device_id=y_peer(k), device_id_type=MESH,
        )

    def offset_of(n):
        return lax.rem(jnp.where(n == 0, 2, jnp.where(n == 1, 1, jnp.where(n == 2, 3, 0))), 4)

    def y_copy_cols(n):
        k = offset_of(n)
        return pltpu.make_async_remote_copy(
            src_ref=sums.at[n], dst_ref=sums.at[4 + n],
            send_sem=y_send.at[1, n, 0], recv_sem=y_recv.at[1, n, 0],
            device_id=y_peer(k), device_id_type=MESH,
        )

    def mass_copy(it, i, slot):
        return pltpu.make_async_remote_copy(
            src_ref=mass_all.at[it, p], dst_ref=mass_all.at[it, slot],
            send_sem=m_send.at[it, i], recv_sem=m_recv.at[it, slot],
            device_id=(lax.rem(p + i, 8), c), device_id_type=MESH,
        )

    def rows_of(yy, cc):
        return pl.ds(pl.multiple_of(cc * 256 + yy * 64, 64), 64)

    def gather_y(k):
        rows = rows_of(y, core)
        return pltpu.make_async_remote_copy(
            src_ref=unit.at[1, rows], dst_ref=unit.at[1, rows],
            send_sem=g_send.at[k - 1], recv_sem=g_recv.at[k - 1],
            device_id=y_peer(k), device_id_type=MESH,
        )

    def gather_sib(k):
        rows = rows_of(at_y(4 - k), core)
        return pltpu.make_async_remote_copy(
            src_ref=unit.at[1, rows], dst_ref=unit.at[1, rows],
            send_sem=gs_send.at[k], recv_sem=gs_recv.at[k],
            device_id=sibling, device_id_type=MESH,
        )

    for it in range(ITERS):
        last = it + 1 == ITERS

        @pl.loop(0, n_chunks)
        def _(ch):
            if it == 0:
                load_points(ch).wait()
            cols = pl.ds(pl.multiple_of(ch * CHUNK, CHUNK), CHUNK)
            logits = lax.dot_general(
                unit[it], pts[cols, :], (((1,), (1,)), ((), ())), preferred_element_type=F32
            )
            local_max = jnp.max(logits, axis=0, keepdims=True)
            shifted = jnp.exp(logits - local_max)
            total = jnp.sum(shifted, axis=0, keepdims=True)
            expd[:, cols] = shifted
            lse = local_max + jnp.log(total)
            for j in range(CHUNK // 128):
                max_loc[ch, j : j + 1, :] = local_max[:, j * 128 : (j + 1) * 128]
                stat[it, ch, c, j : j + 1, :] = lse[:, j * 128 : (j + 1) * 128]

            @pl.loop(1, 16)
            def _(i):
                stat_copy(it, ch, i, c).start()

        mass[...] = jnp.zeros_like(mass)

        @pl.loop(0, n_chunks)
        def _(ch):
            @pl.loop(1, 16)
            def _(i):
                stat_copy(it, ch, i, lax.rem(c + i, 16)).wait_recv()

            every = stat[it, ch]
            row_max = jnp.max(every, axis=0)
            lse = row_max + jnp.log(jnp.sum(jnp.exp(every - row_max[None]), axis=0))
            if last:
                log_out[pl.ds(pl.multiple_of(ch * 8, 8), 8), :] = lse
            scale = jnp.exp(max_loc[ch] - lse)
            for half in range(2):
                part = None
                for j in range(half * 4, half * 4 + 4):
                    cols = pl.ds(pl.multiple_of(ch * CHUNK + j * 128, 128), 128)
                    weights = (expd[:, cols] * scale[j : j + 1, :]).astype(BF16)
                    wts[:, cols] = weights
                    wide = weights.astype(F32)
                    part = wide if part is None else part + wide
                mass[...] += part

        for b in range(4):
            block = mass[b * 128 : (b + 1) * 128, :].T
            mass_all[it, p, :, b * 128 : (b + 1) * 128] = jnp.broadcast_to(
                jnp.sum(block, axis=0, keepdims=True), (8, 128)
            )

        @pl.loop(1, 8)
        def _(i):
            mass_copy(it, i, p).start()

        def finish_pair(n):
            sib_copy(it, n).wait_recv()
            if not last:
                pair[n] = acc[it, n, pl.ds(pl.multiple_of(core * 256, 256), 256), :] + sib_buf[n]
                for k in (2, 1, 3):
                    y_copy_rows(n, k).start()
            else:
                sums[n] = acc[it, n, :, pl.ds(pl.multiple_of(core * 128, 128), 128)] + col_buf[n]

                @pl.when(n < 3)
                def _():
                    y_copy_cols(n).start()

        @pl.loop(0, n_cols)
        def _(n):
            j = at_y(offset_of(n)) if last else n
            cols = pl.ds(pl.multiple_of(j * COLS, COLS), COLS)
            acc[it, n] = jnp.dot(wts[...], pts[:, cols], preferred_element_type=F32)
            sib_copy(it, n).start()

            @pl.when(n > 0)
            def _():
                finish_pair(n - 1)

        finish_pair(n_cols - 1)

        @pl.loop(1, 8)
        def _(i):
            mass_copy(it, i, lax.rem(p + i, 8)).wait_recv()

        total_mass = jnp.sum(mass_all[it], axis=0)
        for b in range(4):
            wide = jnp.broadcast_to(total_mass[0:1, b * 128 : (b + 1) * 128], (128, 128))
            mass_col[b * 128 : (b + 1) * 128, :] = jnp.maximum(wide.T, 1.0)

        if not last:
            own = rows_of(y, core)
            own_half = pl.ds(pl.multiple_of(y * 64, 64), 64)
            divisor = mass_col[own, :]
            squares = jnp.zeros((64, 128), F32)
            for n in range(n_cols):
                for k in (1, 3, 2):
                    y_copy_rows(n, k).wait_recv()
                v = pair[n, own_half, :] + y_buf[n, 0] + y_buf[n, 1] + y_buf[n, 2]
                for h in range(COLS // 128):
                    q = v[:, h * 128 : (h + 1) * 128] / divisor
                    cen[0:64, n * COLS + h * 128 : n * COLS + (h + 1) * 128] = q
                    squares = squares + q * q
            norm = lax.rsqrt(jnp.sum(squares, axis=1, keepdims=True) + 1e-06)
            unit[1, own, :] = (cen[0:64, :] * norm).astype(BF16)
            for k in (2, 1, 3):
                gather_y(k).start()
            gather_sib(0).start()
            for k in (1, 3, 2):
                gather_y(k).wait_recv()
                gather_sib(k).start()
            for k in range(4):
                gather_sib(k).wait_recv()
        else:
            result = sums[3]
            for n in (1, 2, 0):
                y_copy_cols(n).wait_recv()
                result = result + sums[4 + n]
            means_out[...] = result / mass_col[...]

    for it in range(ITERS):

        @pl.loop(0, n_chunks)
        def _(ch):
            @pl.loop(1, 16)
            def _(i):
                stat_copy(it, ch, i, c).wait_send()

        @pl.loop(1, 8)
        def _(i):
            mass_copy(it, i, p).wait_send()

        @pl.loop(0, n_cols)
        def _(n):
            sib_copy(it, n).wait_send()

    for k in (1, 2, 3):
        gather_y(k).wait_send()
        y_copy_cols(k - 1).wait_send()

        @pl.loop(0, n_cols)
        def _(n):
            y_copy_rows(n, k).wait_send()

    for k in range(4):
        gather_sib(k).wait_send()


def on_device(points, centroids):
    n_pts, depth = points.shape
    rows = centroids.shape[0]
    n_chunks, n_cols = n_pts // CHUNK, depth // COLS
    vmem, dma = pltpu.VMEM, pltpu.SemaphoreType.DMA
    means, logs = pl.pallas_call(
        kernel,
        out_shape=(
            jax.ShapeDtypeStruct((rows, 128), F32),
            jax.ShapeDtypeStruct((n_pts // 128, 128), F32),
        ),
        in_specs=[pl.BlockSpec(memory_space=pl.ANY)] * 2,
        out_specs=(pl.BlockSpec(memory_space=pltpu.VMEM),) * 2,
        scratch_shapes=[
            vmem((n_pts, depth), BF16),
            vmem((rows, depth), F32),
            vmem((2, rows, depth), BF16),
            vmem((rows, n_pts), F32),
            vmem((rows, n_pts), BF16),
            vmem((rows, 128), F32),
            vmem((n_chunks, 8, 128), F32),
            vmem((2, n_chunks, 16, 8, 128), F32),
            vmem((2, n_cols, rows, COLS), F32),
            vmem((n_cols, rows // 2, COLS), F32),
            vmem((n_cols, rows // 2, COLS), F32),
            vmem((n_cols, 3, rows // 8, COLS), F32),
            vmem((n_cols, rows, 128), F32),
            vmem((2, 8, 8, rows), F32),
            vmem((rows, 128), F32),
            vmem((7, rows, 128), F32),
            dma((n_chunks + 1,)),
            dma((2, n_chunks, 16)), dma((2, n_chunks, 16)),
            dma((2, n_cols)), dma((2, n_cols)),
            dma((2, n_cols, 3)), dma((2, n_cols, 3)),
            dma((2, 8)), dma((2, 8)),
            dma((3,)), dma((3,)),
            dma((4,)), dma((4,)),
        ],
        compiler_params=pltpu.CompilerParams(
            collective_id=0, has_side_effects=True, vmem_limit_bytes=62 * 1024 * 1024
        ),
        name="kmeans",
    )(points, centroids)
    return means, logs.reshape(n_pts)


def solution(mesh):
    return jax.shard_map(
        on_device,
        mesh=mesh,
        in_specs=(P("pts", None), P("cen", None)),
        out_specs=(P("cen", "pts"), P("pts")),
        check_vma=False,
    )
```

```python
import functools
import jax
import jax.numpy as jnp
from jax import lax
from jax.experimental import pallas as pl
from jax.experimental.pallas import tpu as pltpu
from jax.sharding import PartitionSpec as P

ITERS = 2
MESH = pl.DeviceIdType.MESH
F32 = jnp.float32
BF16 = jnp.bfloat16
CHUNK = 1024
COLS = 256


OCTAVES = 24.0
HALF = 117.0
STEPS = 2.0 * HALF / OCTAVES


def encode(ratio):
    u = jnp.maximum(jnp.log2(jnp.abs(ratio)) + OCTAVES, 0.0) * STEPS
    upper = jnp.floor(u)
    value = jnp.exp2(upper - HALF) * (1.0 + (u - upper))
    return jnp.where(ratio < 0.0, -value, value).astype(BF16)


def decode(code):
    value = code.astype(F32)
    size = jnp.abs(value)
    upper = jnp.floor(jnp.log2(size) + 0.004)
    u = upper + (HALF - 1.0) + size * jnp.exp2(-upper)
    ratio = jnp.exp2(u * (1.0 / STEPS) - OCTAVES)
    ratio = jnp.where(u < 0.004, 0.0, ratio)
    return jnp.where(value < 0.0, -ratio, ratio)


def kernel(
    pts_hbm, cen_hbm, means_out, log_out,
    pts, cen, unit, expd, wts, mass, max_loc, stat, acc, pair, sib_buf, row_code, row_got, col_buf,
    col_code, col_got, mass_all, inverse, bounds, mass_col,
    in_sem, st_send, st_recv, sib_send, sib_recv, y_send, y_recv, m_send, m_recv,
    g_send, g_recv, gs_send, gs_recv,
):
    p = lax.axis_index("pts")
    c = lax.axis_index("cen")
    y, core = p // 2, lax.rem(p, 2)
    other = 1 - core
    n_chunks = pts.shape[0] // CHUNK
    n_cols = pts.shape[1] // COLS

    def at_y(k):
        return lax.rem(y + k, 4)

    def y_peer(k):
        return (at_y(k) * 2 + core, c)

    sib_index = y * 2 + other
    sibling = (sib_index, c)

    def load_points(i):
        rows = pl.ds(pl.multiple_of(i * CHUNK, CHUNK), CHUNK)
        return pltpu.make_async_copy(pts_hbm.at[rows], pts.at[rows], in_sem.at[i])

    load_cen = pltpu.make_async_copy(cen_hbm, cen, in_sem.at[n_chunks])
    load_cen.start()

    @pl.loop(0, n_chunks)
    def _(i):
        load_points(i).start()

    barrier = pltpu.get_barrier_semaphore()

    @pl.loop(1, 16)
    def _(i):
        pl.semaphore_signal(barrier, inc=1, device_id=(p, lax.rem(c + i, 16)), device_id_type=MESH)

    @pl.loop(1, 8)
    def _(i):
        pl.semaphore_signal(barrier, inc=1, device_id=(lax.rem(p + i, 8), c), device_id_type=MESH)

    load_cen.wait()

    @pl.loop(0, 8)
    def _(b):
        rows = pl.ds(pl.multiple_of(b * 64, 64), 64)
        v = cen[rows, :]
        squares = jnp.sum(v * v, axis=1, keepdims=True)
        unit[0, rows, :] = (v * lax.rsqrt(squares + 1e-06)).astype(BF16)

    def stat_copy(it, ch, i, slot):
        return pltpu.make_async_remote_copy(
            src_ref=stat.at[it, ch, c], dst_ref=stat.at[it, ch, slot],
            send_sem=st_send.at[it, ch, i], recv_sem=st_recv.at[it, ch, slot],
            device_id=(p, lax.rem(c + i, 16)), device_id_type=MESH,
        )

    def sib_copy(it, n):
        if it == 0:
            src = acc.at[it, n, pl.ds(pl.multiple_of(other * 256, 256), 256), :]
            dst = sib_buf.at[n]
        else:
            src = acc.at[it, n, :, pl.ds(pl.multiple_of(other * 128, 128), 128)]
            dst = col_buf.at[n]
        return pltpu.make_async_remote_copy(
            src_ref=src, dst_ref=dst, send_sem=sib_send.at[it, n], recv_sem=sib_recv.at[it, n],
            device_id=sibling, device_id_type=MESH,
        )

    def y_copy_rows(n, k):
        return pltpu.make_async_remote_copy(
            src_ref=row_code.at[n, k - 1], dst_ref=row_got.at[n, k - 1],
            send_sem=y_send.at[0, n, k - 1], recv_sem=y_recv.at[0, n, k - 1],
            device_id=y_peer(k), device_id_type=MESH,
        )

    def offset_of(n):
        return lax.rem(jnp.where(n == 0, 2, jnp.where(n == 1, 1, jnp.where(n == 2, 3, 0))), 4)

    def y_copy_cols(n):
        k = offset_of(n)
        return pltpu.make_async_remote_copy(
            src_ref=col_code.at[n], dst_ref=col_got.at[n],
            send_sem=y_send.at[1, n, 0], recv_sem=y_recv.at[1, n, 0],
            device_id=y_peer(k), device_id_type=MESH,
        )

    def mass_copy(it, i, slot):
        return pltpu.make_async_remote_copy(
            src_ref=mass_all.at[it, p], dst_ref=mass_all.at[it, slot],
            send_sem=m_send.at[it, i], recv_sem=m_recv.at[it, slot],
            device_id=(lax.rem(p + i, 8), c), device_id_type=MESH,
        )

    def rows_of(yy, cc):
        return pl.ds(pl.multiple_of(cc * 256 + yy * 64, 64), 64)

    def gather_y(k):
        rows = rows_of(y, core)
        return pltpu.make_async_remote_copy(
            src_ref=unit.at[1, rows], dst_ref=unit.at[1, rows],
            send_sem=g_send.at[k - 1], recv_sem=g_recv.at[k - 1],
            device_id=y_peer(k), device_id_type=MESH,
        )

    def gather_sib(k):
        rows = rows_of(at_y(4 - k), core)
        return pltpu.make_async_remote_copy(
            src_ref=unit.at[1, rows], dst_ref=unit.at[1, rows],
            send_sem=gs_send.at[k], recv_sem=gs_recv.at[k],
            device_id=sibling, device_id_type=MESH,
        )

    for it in range(ITERS):
        last = it + 1 == ITERS

        @pl.loop(0, n_chunks)
        def _(ch):
            if it == 0:
                load_points(ch).wait()
            cols = pl.ds(pl.multiple_of(ch * CHUNK, CHUNK), CHUNK)
            logits = lax.dot_general(
                unit[it], pts[cols, :], (((1,), (1,)), ((), ())), preferred_element_type=F32
            )
            local_max = jnp.max(logits, axis=0, keepdims=True)
            shifted = jnp.exp(logits - local_max)
            total = jnp.sum(shifted, axis=0, keepdims=True)
            expd[:, cols] = shifted
            lse = local_max + jnp.log(total)
            for j in range(CHUNK // 128):
                max_loc[ch, j : j + 1, :] = local_max[:, j * 128 : (j + 1) * 128]
                stat[it, ch, c, j : j + 1, :] = lse[:, j * 128 : (j + 1) * 128]

            if it == 0:

                @pl.when(ch == 0)
                def _():
                    pl.semaphore_wait(barrier, 22)

            @pl.loop(1, 16)
            def _(i):
                stat_copy(it, ch, i, c).start()

        mass[...] = jnp.zeros_like(mass)

        if it == 0:
            def largest(i, so_far):
                block = pts[pl.ds(pl.multiple_of(i * 128, 128), 128), :]
                return jnp.maximum(so_far, jnp.abs(block).reshape(8, 16, pts.shape[1]).max(axis=0))

            tile = lax.fori_loop(
                0, pts.shape[0] // 128, largest, jnp.zeros((16, pts.shape[1]), BF16)
            )
            size_bound = jnp.max(jnp.max(tile.astype(F32), axis=0, keepdims=True), axis=1, keepdims=True)

        def weigh(ch):
            @pl.loop(1, 16)
            def _(i):
                stat_copy(it, ch, i, lax.rem(c + i, 16)).wait_recv()

            every = stat[it, ch]
            row_max = jnp.max(every, axis=0)
            lse = row_max + jnp.log(jnp.sum(jnp.exp(every - row_max[None]), axis=0))
            if last:
                log_out[pl.ds(pl.multiple_of(ch * 8, 8), 8), :] = lse
            scale = jnp.exp(max_loc[ch] - lse)
            for half in range(2):
                part = None
                for j in range(half * 4, half * 4 + 4):
                    cols = pl.ds(pl.multiple_of(ch * CHUNK + j * 128, 128), 128)
                    weights = (expd[:, cols] * scale[j : j + 1, :]).astype(BF16)
                    wts[:, cols] = weights
                    wide = weights.astype(F32)
                    part = wide if part is None else part + wide
                mass[...] += part

        early = (n_chunks - 1) * CHUNK

        @pl.loop(0, n_chunks - 1)
        def _(ch):
            weigh(ch)

        def columns(n):
            j = at_y(offset_of(n)) if last else n
            return pl.ds(pl.multiple_of(j * COLS, COLS), COLS)

        @pl.loop(0, n_cols)
        def _(n):
            acc[it, n] = jnp.dot(
                wts[:, 0:early], pts[0:early, columns(n)], preferred_element_type=F32
            )

        weigh(n_chunks - 1)

        for b in range(4):
            block = mass[b * 128 : (b + 1) * 128, :].T
            mass_all[it, p, 0:1, b * 128 : (b + 1) * 128] = jnp.sum(block, axis=0, keepdims=True)
        mass_all[it, p, 1:2, :] = jnp.broadcast_to(size_bound[0:1, 0:1], (1, pair.shape[1] * 2))

        @pl.loop(1, 8)
        def _(i):
            mass_copy(it, i, p).start()

        def chip_mass(yy):
            row = mass_all[it, yy * 2, 0:1, :] + mass_all[it, yy * 2 + 1, 0:1, :]
            size = jnp.maximum(mass_all[it, yy * 2, 1:2, :], mass_all[it, yy * 2 + 1, 1:2, :])
            return row, jnp.maximum(row * size, 1e-30)

        def down(row, b):
            return jnp.broadcast_to(row[:, b * 128 : (b + 1) * 128], (128, 128)).T

        def finish_pair(n):
            sib_copy(it, n).wait_recv()
            if not last:
                half = pl.multiple_of(core * 256, 256)
                pair[n] = acc[it, n, pl.ds(half, 256), :] + sib_buf[n]
                for k in (2, 1, 3):
                    at = pl.multiple_of(at_y(k) * 64, 64)
                    for h in range(COLS // 128):
                        lanes = slice(h * 128, (h + 1) * 128)
                        row_code[n, k - 1, :, lanes] = encode(
                            pair[n, pl.ds(at, 64), lanes] * inverse[pl.ds(half + at, 64), :]
                        )
                    y_copy_rows(n, k).start()
            else:
                sums = acc[it, n, :, pl.ds(pl.multiple_of(core * 128, 128), 128)] + col_buf[n]
                if isinstance(n, int):
                    return sums
                col_code[n] = encode(sums * inverse[...])
                y_copy_cols(n).start()

        def finish_columns(n):
            acc[it, n] += jnp.dot(
                wts[:, early:], pts[early:, columns(n)], preferred_element_type=F32
            )
            sib_copy(it, n).start()

        finish_columns(0)
        mass_copy(it, lax.rem(8 + other - core, 8), sib_index).wait_recv()
        _, bound = chip_mass(y)
        for b in range(4):
            inverse[b * 128 : (b + 1) * 128, :] = down(1.0 / bound, b)

        @pl.loop(1, n_cols)
        def _(n):
            finish_columns(n)
            finish_pair(n - 1)

        own_sum = finish_pair(n_cols - 1)

        @pl.loop(1, 8)
        def _(i):
            @pl.when(lax.rem(p + i, 8) != sib_index)
            def _():
                mass_copy(it, i, lax.rem(p + i, 8)).wait_recv()

        total_mass, _ = chip_mass(y)
        for k in range(1, 4):
            row, bound = chip_mass(at_y(4 - k))
            total_mass = total_mass + row
            for b in range(4):
                bounds[k - 1, b * 128 : (b + 1) * 128, :] = down(bound, b)
        for b in range(4):
            mass_col[b * 128 : (b + 1) * 128, :] = jnp.maximum(down(total_mass, b), 1.0)

        if not last:
            own = rows_of(y, core)
            own_half = pl.ds(pl.multiple_of(y * 64, 64), 64)
            divisor = mass_col[own, :]
            squares = jnp.zeros((64, 128), F32)
            for n in range(n_cols):
                for k in (1, 3, 2):
                    y_copy_rows(n, k).wait_recv()
                for h in range(COLS // 128):
                    lanes = slice(h * 128, (h + 1) * 128)
                    v = pair[n, own_half, lanes]
                    for k in range(1, 4):
                        v = v + decode(row_got[n, k - 1, :, lanes]) * bounds[k - 1, own, :]
                    q = v / divisor
                    cen[0:64, n * COLS + h * 128 : n * COLS + (h + 1) * 128] = q
                    squares = squares + q * q
            norm = lax.rsqrt(jnp.sum(squares, axis=1, keepdims=True) + 1e-06)
            unit[1, own, :] = (cen[0:64, :] * norm).astype(BF16)
            for k in (2, 1, 3):
                gather_y(k).start()
            gather_sib(0).start()
            for k in (1, 3, 2):
                gather_y(k).wait_recv()
                gather_sib(k).start()
            for k in range(4):
                gather_sib(k).wait_recv()
        else:
            result = own_sum
            for n, k in ((1, 1), (2, 3), (0, 2)):
                y_copy_cols(n).wait_recv()
                result = result + decode(col_got[n]) * bounds[k - 1]
            means_out[...] = result / mass_col[...]

    for it in range(ITERS):

        @pl.loop(0, n_chunks)
        def _(ch):
            @pl.loop(1, 16)
            def _(i):
                stat_copy(it, ch, i, c).wait_send()

        @pl.loop(1, 8)
        def _(i):
            mass_copy(it, i, p).wait_send()

        @pl.loop(0, n_cols)
        def _(n):
            sib_copy(it, n).wait_send()

    for k in (1, 2, 3):
        gather_y(k).wait_send()
        y_copy_cols(k - 1).wait_send()

        @pl.loop(0, n_cols)
        def _(n):
            y_copy_rows(n, k).wait_send()

    for k in range(4):
        gather_sib(k).wait_send()


def write_out(means, logs, means_out, log_out):
    means_out[...] = means[...]
    log_out[...] = logs[...]


def on_device(points, centroids):
    n_pts, depth = points.shape
    rows = centroids.shape[0]
    n_chunks, n_cols = n_pts // CHUNK, depth // COLS
    vmem, dma = pltpu.VMEM, pltpu.SemaphoreType.DMA
    means, logs = pl.pallas_call(
        kernel,
        out_shape=(
            jax.ShapeDtypeStruct((rows, 128), F32),
            jax.ShapeDtypeStruct((n_pts // 128, 128), F32),
        ),
        in_specs=[pl.BlockSpec(memory_space=pl.ANY)] * 2,
        out_specs=(pl.BlockSpec(memory_space=pltpu.VMEM),) * 2,
        scratch_shapes=[
            vmem((n_pts, depth), BF16),
            vmem((rows, depth), F32),
            vmem((2, rows, depth), BF16),
            vmem((rows, n_pts), F32),
            vmem((rows, n_pts), BF16),
            vmem((rows, 128), F32),
            vmem((n_chunks, 8, 128), F32),
            vmem((2, n_chunks, 16, 8, 128), F32),
            vmem((2, n_cols, rows, COLS), F32),
            vmem((n_cols, rows // 2, COLS), F32),
            vmem((n_cols, rows // 2, COLS), F32),
            vmem((n_cols, 3, rows // 8, COLS), BF16),
            vmem((n_cols, 3, rows // 8, COLS), BF16),
            vmem((n_cols, rows, 128), F32),
            vmem((3, rows, 128), BF16),
            vmem((3, rows, 128), BF16),
            vmem((2, 8, 8, rows), F32),
            vmem((rows, 128), F32),
            vmem((3, rows, 128), F32),
            vmem((rows, 128), F32),
            dma((n_chunks + 1,)),
            dma((2, n_chunks, 16)), dma((2, n_chunks, 16)),
            dma((2, n_cols)), dma((2, n_cols)),
            dma((2, n_cols, 3)), dma((2, n_cols, 3)),
            dma((2, 8)), dma((2, 8)),
            dma((3,)), dma((3,)),
            dma((4,)), dma((4,)),
        ],
        compiler_params=pltpu.CompilerParams(
            collective_id=0, has_side_effects=True, vmem_limit_bytes=62 * 1024 * 1024
        ),
        name="kmeans",
    )(points, centroids)
    means, logs = pl.pallas_call(
        write_out,
        out_shape=(
            jax.ShapeDtypeStruct(means.shape, F32), jax.ShapeDtypeStruct(logs.shape, F32),
        ),
        in_specs=[pl.BlockSpec(memory_space=pltpu.VMEM)] * 2,
        out_specs=(pl.BlockSpec(memory_space=pltpu.VMEM),) * 2,
        name="write_out",
    )(means, logs)
    return means, logs.reshape(n_pts)


def solution(mesh):
    return jax.shard_map(
        on_device,
        mesh=mesh,
        in_specs=(P("pts", None), P("cen", None)),
        out_specs=(P("cen", "pts"), P("pts")),
        check_vma=False,
    )
```

```python
import functools
import jax
import jax.numpy as jnp
from jax import lax
from jax.experimental import pallas as pl
from jax.experimental.pallas import tpu as pltpu
from jax.sharding import PartitionSpec as P

ITERS = 2
MESH = pl.DeviceIdType.MESH
F32 = jnp.float32
BF16 = jnp.bfloat16
CHUNK = 1024
COLS = 256


OCTAVES = 24.0
HALF = 117.0
STEPS = 2.0 * HALF / OCTAVES


def encode(ratio):
    u = jnp.maximum(jnp.log2(jnp.abs(ratio)) + OCTAVES, 0.0) * STEPS
    upper = jnp.floor(u)
    value = jnp.exp2(upper - HALF) * (1.0 + (u - upper))
    return jnp.where(ratio < 0.0, -value, value).astype(BF16)


def decode(code):
    value = code.astype(F32)
    size = jnp.abs(value)
    upper = jnp.floor(jnp.log2(size) + 0.004)
    u = upper + (HALF - 1.0) + size * jnp.exp2(-upper)
    ratio = jnp.exp2(u * (1.0 / STEPS) - OCTAVES)
    ratio = jnp.where(u < 0.004, 0.0, ratio)
    return jnp.where(value < 0.0, -ratio, ratio)


def kernel(
    pts_hbm, cen_hbm, means_out, log_out,
    pts, cen, unit, expd, wts, mass, max_loc, stat, acc, pair, sib_buf, row_code, row_got, col_buf,
    col_code, col_got, mass_all, inverse, bounds, mass_col,
    in_sem, st_send, st_recv, sib_send, sib_recv, y_send, y_recv, m_send, m_recv,
    g_send, g_recv, gs_send, gs_recv,
):
    p = lax.axis_index("pts")
    c = lax.axis_index("cen")
    y, core = p // 2, lax.rem(p, 2)
    other = 1 - core
    n_chunks = pts.shape[0] // CHUNK
    n_cols = pts.shape[1] // COLS

    def at_y(k):
        return lax.rem(y + k, 4)

    def y_peer(k):
        return (at_y(k) * 2 + core, c)

    sib_index = y * 2 + other
    sibling = (sib_index, c)

    def load_points(i):
        rows = pl.ds(pl.multiple_of(i * CHUNK, CHUNK), CHUNK)
        return pltpu.make_async_copy(pts_hbm.at[rows], pts.at[rows], in_sem.at[i])

    load_cen = pltpu.make_async_copy(cen_hbm, cen, in_sem.at[n_chunks])
    load_cen.start()

    @pl.loop(0, n_chunks)
    def _(i):
        load_points(i).start()

    barrier = pltpu.get_barrier_semaphore()

    @pl.loop(1, 16)
    def _(i):
        pl.semaphore_signal(barrier, inc=1, device_id=(p, lax.rem(c + i, 16)), device_id_type=MESH)

    @pl.loop(1, 8)
    def _(i):
        pl.semaphore_signal(barrier, inc=1, device_id=(lax.rem(p + i, 8), c), device_id_type=MESH)

    load_cen.wait()

    @pl.loop(0, 8)
    def _(b):
        rows = pl.ds(pl.multiple_of(b * 64, 64), 64)
        v = cen[rows, :]
        squares = jnp.sum(v * v, axis=1, keepdims=True)
        unit[0, rows, :] = (v * lax.rsqrt(squares + 1e-06)).astype(BF16)

    def stat_copy(it, ch, i, slot):
        return pltpu.make_async_remote_copy(
            src_ref=stat.at[it, ch, c], dst_ref=stat.at[it, ch, slot],
            send_sem=st_send.at[it, ch], recv_sem=st_recv.at[it, ch],
            device_id=(p, lax.rem(c + i, 16)), device_id_type=MESH,
        )

    def offset_of(n):
        return lax.rem(jnp.where(n == 0, 2, jnp.where(n == 1, 1, jnp.where(n == 2, 3, 0))), 4)

    def all_stats(it, ch):
        some = stat.at[it, ch, pl.ds(0, 15)]
        return pltpu.make_async_remote_copy(
            src_ref=some, dst_ref=some, send_sem=st_send.at[it, ch], recv_sem=st_recv.at[it, ch],
            device_id=sibling, device_id_type=MESH,
        )

    def sib_copy(it, n):
        if it == 0:
            src = acc.at[it, n, pl.ds(pl.multiple_of(other * 256, 256), 256), :]
            dst = sib_buf.at[n]
        else:
            src = acc.at[it, at_y(offset_of(n)), :, pl.ds(pl.multiple_of(other * 128, 128), 128)]
            dst = col_buf.at[n]
        return pltpu.make_async_remote_copy(
            src_ref=src, dst_ref=dst, send_sem=sib_send.at[it, n], recv_sem=sib_recv.at[it, n],
            device_id=sibling, device_id_type=MESH,
        )

    def y_copy_rows(n, k):
        return pltpu.make_async_remote_copy(
            src_ref=row_code.at[n, k - 1], dst_ref=row_got.at[n, k - 1],
            send_sem=y_send.at[0, n, k - 1], recv_sem=y_recv.at[0, n, k - 1],
            device_id=y_peer(k), device_id_type=MESH,
        )

    def y_copy_cols(n):
        k = offset_of(n)
        return pltpu.make_async_remote_copy(
            src_ref=col_code.at[n], dst_ref=col_got.at[n],
            send_sem=y_send.at[1, n, 0], recv_sem=y_recv.at[1, n, 0],
            device_id=y_peer(k), device_id_type=MESH,
        )

    def all_masses(it, some, sem):
        some = mass_all.at[it, pl.ds(0, some)]
        return pltpu.make_async_remote_copy(
            src_ref=some, dst_ref=some, send_sem=m_send.at[it], recv_sem=m_recv.at[it, sem],
            device_id=sibling, device_id_type=MESH,
        )

    def mass_copy(it, i, slot, sem):
        return pltpu.make_async_remote_copy(
            src_ref=mass_all.at[it, p], dst_ref=mass_all.at[it, slot],
            send_sem=m_send.at[it], recv_sem=m_recv.at[it, sem],
            device_id=(lax.rem(p + i, 8), c), device_id_type=MESH,
        )

    def rows_of(yy, cc):
        return pl.ds(pl.multiple_of(cc * 256 + yy * 64, 64), 64)

    def gather_y(k):
        rows = rows_of(y, core)
        return pltpu.make_async_remote_copy(
            src_ref=unit.at[1, rows], dst_ref=unit.at[1, rows],
            send_sem=g_send.at[k - 1], recv_sem=g_recv.at[k - 1],
            device_id=y_peer(k), device_id_type=MESH,
        )

    def gather_sib(k):
        rows = rows_of(at_y(4 - k), core)
        return pltpu.make_async_remote_copy(
            src_ref=unit.at[1, rows], dst_ref=unit.at[1, rows],
            send_sem=gs_send.at[k], recv_sem=gs_recv.at[k],
            device_id=sibling, device_id_type=MESH,
        )

    for it in range(ITERS):
        last = it + 1 == ITERS

        @pl.loop(0, n_chunks)
        def _(ch):
            if it == 0:
                load_points(ch).wait()
            cols = pl.ds(pl.multiple_of(ch * CHUNK, CHUNK), CHUNK)
            logits = lax.dot_general(
                unit[it], pts[cols, :], (((1,), (1,)), ((), ())), preferred_element_type=F32
            )
            local_max = jnp.max(logits, axis=0, keepdims=True)
            shifted = jnp.exp(logits - local_max)
            total = jnp.sum(shifted, axis=0, keepdims=True)
            expd[:, cols] = shifted
            lse = local_max + jnp.log(total)
            for j in range(CHUNK // 128):
                max_loc[ch, j : j + 1, :] = local_max[:, j * 128 : (j + 1) * 128]
                stat[it, ch, c, j : j + 1, :] = lse[:, j * 128 : (j + 1) * 128]

            if it == 0:

                @pl.when(ch == 0)
                def _():
                    pl.semaphore_wait(barrier, 22)

            @pl.loop(1, 16)
            def _(i):
                stat_copy(it, ch, i, c).start()

        mass[...] = jnp.zeros_like(mass)

        if it == 0:
            def largest(i, so_far):
                block = pts[pl.ds(pl.multiple_of(i * 128, 128), 128), :]
                return jnp.maximum(so_far, jnp.abs(block).reshape(8, 16, pts.shape[1]).max(axis=0))

            tile = lax.fori_loop(
                0, pts.shape[0] // 128, largest, jnp.zeros((16, pts.shape[1]), BF16)
            )
            size_bound = jnp.max(jnp.max(tile.astype(F32), axis=0, keepdims=True), axis=1, keepdims=True)

        def weigh(ch):
            all_stats(it, ch).wait_recv()
            every = stat[it, ch]
            row_max = jnp.max(every, axis=0)
            lse = row_max + jnp.log(jnp.sum(jnp.exp(every - row_max[None]), axis=0))
            if last:
                log_out[pl.ds(pl.multiple_of(ch * 8, 8), 8), :] = lse
            scale = jnp.exp(max_loc[ch] - lse)
            for half in range(2):
                part = None
                for j in range(half * 4, half * 4 + 4):
                    cols = pl.ds(pl.multiple_of(ch * CHUNK + j * 128, 128), 128)
                    weights = (expd[:, cols] * scale[j : j + 1, :]).astype(BF16)
                    wts[:, cols] = weights
                    wide = weights.astype(F32)
                    part = wide if part is None else part + wide
                mass[...] += part

        early = (n_chunks - 1) * CHUNK

        def slot(n):
            return at_y(offset_of(n)) if last else n

        def columns(n):
            return pl.ds(pl.multiple_of(slot(n) * COLS, COLS), COLS)

        def product(ch):
            cols = pl.ds(pl.multiple_of(ch * CHUNK, CHUNK), CHUNK)
            return jnp.dot(wts[:, cols], pts[cols, :], preferred_element_type=F32)

        weigh(0)
        first = product(0)
        for n in range(n_cols):
            acc[it, n] = first[:, n * COLS : (n + 1) * COLS]

        @pl.loop(1, n_chunks - 1)
        def _(ch):
            weigh(ch)
            more = product(ch)
            for n in range(n_cols):
                acc[it, n] += more[:, n * COLS : (n + 1) * COLS]

        weigh(n_chunks - 1)

        for b in range(4):
            block = mass[b * 128 : (b + 1) * 128, :].T
            mass_all[it, p, 0:1, b * 128 : (b + 1) * 128] = jnp.sum(block, axis=0, keepdims=True)
        mass_all[it, p, 1:2, :] = jnp.broadcast_to(size_bound[0:1, 0:1], (1, pair.shape[1] * 2))

        to_sib = lax.rem(8 + other - core, 8)
        mass_copy(it, to_sib, p, 0).start()

        @pl.loop(1, 8)
        def _(i):
            @pl.when(i != to_sib)
            def _():
                mass_copy(it, i, p, 1).start()

        def chip_mass(yy):
            row = mass_all[it, yy * 2, 0:1, :] + mass_all[it, yy * 2 + 1, 0:1, :]
            size = jnp.maximum(mass_all[it, yy * 2, 1:2, :], mass_all[it, yy * 2 + 1, 1:2, :])
            return row, jnp.maximum(row * size, 1e-30)

        def down(row, b):
            return jnp.broadcast_to(row[:, b * 128 : (b + 1) * 128], (128, 128)).T

        def finish_pair(n):
            sib_copy(it, n).wait_recv()
            if not last:
                half = pl.multiple_of(core * 256, 256)
                pair[n] = acc[it, n, pl.ds(half, 256), :] + sib_buf[n]
                for k in (2, 1, 3):
                    at = pl.multiple_of(at_y(k) * 64, 64)
                    for h in range(COLS // 128):
                        lanes = slice(h * 128, (h + 1) * 128)
                        row_code[n, k - 1, :, lanes] = encode(
                            pair[n, pl.ds(at, 64), lanes] * inverse[pl.ds(half + at, 64), :]
                        )
                    y_copy_rows(n, k).start()
            else:
                sums = acc[it, slot(n), :, pl.ds(pl.multiple_of(core * 128, 128), 128)] + col_buf[n]
                if isinstance(n, int):
                    return sums
                col_code[n] = encode(sums * inverse[...])
                y_copy_cols(n).start()

        def finish_columns(n):
            acc[it, slot(n)] += jnp.dot(
                wts[:, early:], pts[early:, columns(n)], preferred_element_type=F32
            )
            sib_copy(it, n).start()

        finish_columns(0)
        all_masses(it, 1, 0).wait_recv()
        _, bound = chip_mass(y)
        for b in range(4):
            inverse[b * 128 : (b + 1) * 128, :] = down(1.0 / bound, b)

        @pl.loop(1, n_cols)
        def _(n):
            finish_columns(n)
            finish_pair(n - 1)

        own_sum = finish_pair(n_cols - 1)

        all_masses(it, 6, 1).wait_recv()

        total_mass, _ = chip_mass(y)
        for k in range(1, 4):
            row, bound = chip_mass(at_y(4 - k))
            total_mass = total_mass + row
            for b in range(4):
                bounds[k - 1, b * 128 : (b + 1) * 128, :] = down(bound, b)
        for b in range(4):
            mass_col[b * 128 : (b + 1) * 128, :] = jnp.maximum(down(total_mass, b), 1.0)

        if not last:
            own = rows_of(y, core)
            own_half = pl.ds(pl.multiple_of(y * 64, 64), 64)
            divisor = mass_col[own, :]
            squares = jnp.zeros((64, 128), F32)
            for n in range(n_cols):
                for k in (1, 3, 2):
                    y_copy_rows(n, k).wait_recv()
                for h in range(COLS // 128):
                    lanes = slice(h * 128, (h + 1) * 128)
                    v = pair[n, own_half, lanes]
                    for k in range(1, 4):
                        v = v + decode(row_got[n, k - 1, :, lanes]) * bounds[k - 1, own, :]
                    q = v / divisor
                    cen[0:64, n * COLS + h * 128 : n * COLS + (h + 1) * 128] = q
                    squares = squares + q * q
            norm = lax.rsqrt(jnp.sum(squares, axis=1, keepdims=True) + 1e-06)
            unit[1, own, :] = (cen[0:64, :] * norm).astype(BF16)
            for k in (2, 1, 3):
                gather_y(k).start()
            gather_sib(0).start()
            for k in (1, 3, 2):
                gather_y(k).wait_recv()
                gather_sib(k).start()
            for k in range(4):
                gather_sib(k).wait_recv()
        else:
            result = own_sum
            for n, k in ((1, 1), (2, 3), (0, 2)):
                y_copy_cols(n).wait_recv()
                result = result + decode(col_got[n]) * bounds[k - 1]
            means_out[...] = result / mass_col[...]

    for it in range(ITERS):

        @pl.loop(0, n_chunks)
        def _(ch):
            all_stats(it, ch).wait_send()

        all_masses(it, 7, 0).wait_send()

        @pl.loop(0, n_cols)
        def _(n):
            sib_copy(it, n).wait_send()

    for k in (1, 2, 3):
        gather_y(k).wait_send()
        y_copy_cols(k - 1).wait_send()

        @pl.loop(0, n_cols)
        def _(n):
            y_copy_rows(n, k).wait_send()

    for k in range(4):
        gather_sib(k).wait_send()


def write_out(means, logs, means_out, log_out):
    means_out[...] = means[...]
    log_out[...] = logs[...]


def on_device(points, centroids):
    n_pts, depth = points.shape
    rows = centroids.shape[0]
    n_chunks, n_cols = n_pts // CHUNK, depth // COLS
    vmem, dma = pltpu.VMEM, pltpu.SemaphoreType.DMA
    means, logs = pl.pallas_call(
        kernel,
        out_shape=(
            jax.ShapeDtypeStruct((rows, 128), F32),
            jax.ShapeDtypeStruct((n_pts // 128, 128), F32),
        ),
        in_specs=[pl.BlockSpec(memory_space=pl.ANY)] * 2,
        out_specs=(pl.BlockSpec(memory_space=pltpu.VMEM),) * 2,
        scratch_shapes=[
            vmem((n_pts, depth), BF16),
            vmem((rows, depth), F32),
            vmem((2, rows, depth), BF16),
            vmem((rows, n_pts), F32),
            vmem((rows, n_pts), BF16),
            vmem((rows, 128), F32),
            vmem((n_chunks, 8, 128), F32),
            vmem((2, n_chunks, 16, 8, 128), F32),
            vmem((2, n_cols, rows, COLS), F32),
            vmem((n_cols, rows // 2, COLS), F32),
            vmem((n_cols, rows // 2, COLS), F32),
            vmem((n_cols, 3, rows // 8, COLS), BF16),
            vmem((n_cols, 3, rows // 8, COLS), BF16),
            vmem((n_cols, rows, 128), F32),
            vmem((3, rows, 128), BF16),
            vmem((3, rows, 128), BF16),
            vmem((2, 8, 8, rows), F32),
            vmem((rows, 128), F32),
            vmem((3, rows, 128), F32),
            vmem((rows, 128), F32),
            dma((n_chunks + 1,)),
            dma((2, n_chunks)), dma((2, n_chunks)),
            dma((2, n_cols)), dma((2, n_cols)),
            dma((2, n_cols, 3)), dma((2, n_cols, 3)),
            dma((2,)), dma((2, 2)),
            dma((3,)), dma((3,)),
            dma((4,)), dma((4,)),
        ],
        compiler_params=pltpu.CompilerParams(
            collective_id=0, has_side_effects=True, vmem_limit_bytes=62 * 1024 * 1024
        ),
        name="kmeans",
    )(points, centroids)
    means, logs = pl.pallas_call(
        write_out,
        out_shape=(
            jax.ShapeDtypeStruct(means.shape, F32), jax.ShapeDtypeStruct(logs.shape, F32),
        ),
        in_specs=[pl.BlockSpec(memory_space=pltpu.VMEM)] * 2,
        out_specs=(pl.BlockSpec(memory_space=pltpu.VMEM),) * 2,
        name="write_out",
    )(means, logs)
    return means, logs.reshape(n_pts)


def solution(mesh):
    return jax.shard_map(
        on_device,
        mesh=mesh,
        in_specs=(P("pts", None), P("cen", None)),
        out_specs=(P("cen", "pts"), P("pts")),
        check_vma=False,
    )
```

```python
import functools
import jax
import jax.numpy as jnp
from jax import lax
from jax.experimental import pallas as pl
from jax.experimental.pallas import tpu as pltpu
from jax.sharding import PartitionSpec as P

ITERS = 2
VMEM_LIMIT = 52 * 1024 * 1024
MESH = pl.DeviceIdType.MESH
F32 = jnp.float32
BF16 = jnp.bfloat16
CHUNK = 1024
COLS = 256
GROUPS = 4


OCTAVES = 24.0
HALF = 117.0
STEPS = 2.0 * HALF / OCTAVES


def encode(ratio):
    u = jnp.maximum(jnp.log2(jnp.abs(ratio)) + OCTAVES, 0.0) * STEPS
    upper = jnp.floor(u)
    value = jnp.exp2(upper - HALF) * (1.0 + (u - upper))
    return jnp.where(ratio < 0.0, -value, value).astype(BF16)


def decode(code):
    value = code.astype(F32)
    size = jnp.abs(value)
    upper = jnp.floor(jnp.log2(size) + 0.004)
    u = upper + (HALF - 1.0) + size * jnp.exp2(-upper)
    ratio = jnp.exp2(u * (1.0 / STEPS) - OCTAVES)
    ratio = jnp.where(u < 0.004, 0.0, ratio)
    return jnp.where(value < 0.0, -ratio, ratio)


def kernel(
    pts_hbm, cen_hbm, means_out, log_out,
    pts, cen, unit, expd, wts, mass, max_loc, stat, acc_rows, acc, pair, sib_buf, row_code, row_got, means_own, col_buf,
    col_code, col_got, mass_all, inverse, bounds, mass_col,
    in_sem, st_send, st_recv, sib_send, sib_recv, y_send, y_recv, m_send, m_recv,
    g_send, g_recv, gs_send, gs_recv,
):
    p = lax.axis_index("pts")
    c = lax.axis_index("cen")
    y, core = p // 2, lax.rem(p, 2)
    other = 1 - core
    n_chunks = pts.shape[0] // CHUNK
    n_cols = pts.shape[1] // COLS
    half_size, own_size = pair.shape[1], pair.shape[1] // 4

    def at_y(k):
        return lax.rem(y + k, 4)

    def y_peer(k):
        return (at_y(k) * 2 + core, c)

    sib_index = y * 2 + other
    sibling = (sib_index, c)

    def load_points(i):
        rows = pl.ds(pl.multiple_of(i * CHUNK, CHUNK), CHUNK)
        return pltpu.make_async_copy(pts_hbm.at[rows], pts.at[rows], in_sem.at[i])

    def load_cen(b):
        rows = pl.ds(pl.multiple_of(b * 128, 128), 128)
        return pltpu.make_async_copy(cen_hbm.at[rows], cen.at[rows], in_sem.at[n_chunks + b])

    @pl.loop(0, 4)
    def _(b):
        load_cen(b).start()

    @pl.loop(0, n_chunks)
    def _(i):
        load_points(i).start()

    barrier = pltpu.get_barrier_semaphore()

    @pl.loop(1, 16)
    def _(i):
        pl.semaphore_signal(barrier, inc=1, device_id=(p, lax.rem(c + i, 16)), device_id_type=MESH)

    @pl.loop(1, 8)
    def _(i):
        pl.semaphore_signal(barrier, inc=1, device_id=(lax.rem(p + i, 8), c), device_id_type=MESH)

    @pl.loop(0, 4)
    def _(b):
        load_cen(b).wait()
        rows = pl.ds(pl.multiple_of(b * 128, 128), 128)
        v = cen[rows, :]
        squares = jnp.sum(v * v, axis=1, keepdims=True)
        unit[0, rows, :] = (v * lax.rsqrt(squares + 1e-06)).astype(BF16)

    def stat_copy(it, ch, i, slot):
        return pltpu.make_async_remote_copy(
            src_ref=stat.at[it, ch, c], dst_ref=stat.at[it, ch, slot],
            send_sem=st_send.at[it, ch], recv_sem=st_recv.at[it, ch],
            device_id=(p, lax.rem(c + i, 16)), device_id_type=MESH,
        )

    def offset_of(n):
        return lax.rem(jnp.where(n == 0, 2, jnp.where(n == 1, 1, jnp.where(n == 2, 3, 0))), 4)

    def all_stats(it, ch):
        some = stat.at[it, ch, pl.ds(0, 15)]
        return pltpu.make_async_remote_copy(
            src_ref=some, dst_ref=some, send_sem=st_send.at[it, ch], recv_sem=st_recv.at[it, ch],
            device_id=sibling, device_id_type=MESH,
        )

    def half_rows(g, cc):
        return pl.ds(pl.multiple_of(g * 2 * half_size + cc * half_size, half_size), half_size)

    def own_rows(g, yy, cc):
        return pl.ds(pl.multiple_of(g * 2 * half_size + cc * half_size + yy * own_size, own_size), own_size)

    def sib_copy(it, n):
        if it == 0:
            src, dst = acc_rows.at[half_rows(n, other)], sib_buf.at[n]
        else:
            src = acc.at[at_y(offset_of(n)), :, pl.ds(pl.multiple_of(other * 128, 128), 128)]
            dst = col_buf.at[n]
        return pltpu.make_async_remote_copy(
            src_ref=src, dst_ref=dst, send_sem=sib_send.at[it, n], recv_sem=sib_recv.at[it, n],
            device_id=sibling, device_id_type=MESH,
        )

    def y_copy_rows(n, k):
        return pltpu.make_async_remote_copy(
            src_ref=row_code.at[n, k - 1], dst_ref=row_got.at[n, k - 1],
            send_sem=y_send.at[0], recv_sem=y_recv.at[0, n],
            device_id=y_peer(k), device_id_type=MESH,
        )

    def y_copy_cols(n):
        k = offset_of(n)
        return pltpu.make_async_remote_copy(
            src_ref=col_code.at[n], dst_ref=col_got.at[n],
            send_sem=y_send.at[1 + n], recv_sem=y_recv.at[1, n],
            device_id=y_peer(k), device_id_type=MESH,
        )

    def all_masses(it, some, sem):
        some = mass_all.at[it, pl.ds(0, some)]
        return pltpu.make_async_remote_copy(
            src_ref=some, dst_ref=some, send_sem=m_send.at[it], recv_sem=m_recv.at[it, sem],
            device_id=sibling, device_id_type=MESH,
        )

    def mass_copy(it, i, slot, sem):
        return pltpu.make_async_remote_copy(
            src_ref=mass_all.at[it, p], dst_ref=mass_all.at[it, slot],
            send_sem=m_send.at[it], recv_sem=m_recv.at[it, sem],
            device_id=(lax.rem(p + i, 8), c), device_id_type=MESH,
        )

    def all_rows(g):
        return pltpu.make_async_remote_copy(
            src_ref=row_code.at[g], dst_ref=row_got.at[g],
            send_sem=y_send.at[0], recv_sem=y_recv.at[0, g],
            device_id=sibling, device_id_type=MESH,
        )

    def all_sent(sem):
        return pltpu.make_async_remote_copy(
            src_ref=row_code, dst_ref=row_code, send_sem=sem, recv_sem=y_recv.at[0, 0],
            device_id=sibling, device_id_type=MESH,
        )

    def gather_y(g, k):
        rows = own_rows(g, y, core)
        return pltpu.make_async_remote_copy(
            src_ref=unit.at[1, rows], dst_ref=unit.at[1, rows],
            send_sem=g_send.at[0], recv_sem=g_recv.at[g],
            device_id=y_peer(k), device_id_type=MESH,
        )

    def all_gather_y(g):
        return pltpu.make_async_remote_copy(
            src_ref=row_code.at[g], dst_ref=row_got.at[g],
            send_sem=g_send.at[0], recv_sem=g_recv.at[g],
            device_id=sibling, device_id_type=MESH,
        )

    def gather_sib(g):
        rows = half_rows(g, core)
        return pltpu.make_async_remote_copy(
            src_ref=unit.at[1, rows], dst_ref=unit.at[1, rows],
            send_sem=gs_send.at[g], recv_sem=gs_recv.at[g],
            device_id=sibling, device_id_type=MESH,
        )

    def sent(it):
        @pl.loop(0, n_chunks)
        def _(ch):
            all_stats(it, ch).wait_send()

        all_masses(it, 7, 0).wait_send()

        @pl.loop(0, n_cols)
        def _(n):
            sib_copy(it, n).wait_send()

    for it in range(ITERS):
        last = it + 1 == ITERS

        @pl.loop(0, n_chunks)
        def _(ch):
            if it == 0:
                load_points(ch).wait()
            cols = pl.ds(pl.multiple_of(ch * CHUNK, CHUNK), CHUNK)
            logits = lax.dot_general(
                unit[it], pts[cols, :], (((1,), (1,)), ((), ())), preferred_element_type=F32
            )
            local_max = jnp.max(logits, axis=0, keepdims=True)
            shifted = jnp.exp(logits - local_max)
            total = jnp.sum(shifted, axis=0, keepdims=True)
            expd[:, cols] = shifted
            lse = local_max + jnp.log(total)
            for j in range(CHUNK // 128):
                max_loc[ch, j : j + 1, :] = local_max[:, j * 128 : (j + 1) * 128]
                stat[it, ch, c, j : j + 1, :] = lse[:, j * 128 : (j + 1) * 128]

            if it == 0:

                @pl.when(ch == 0)
                def _():
                    pl.semaphore_wait(barrier, 22)

            for i in range(1, 16):
                stat_copy(it, ch, i, c).start()

        mass[...] = jnp.zeros_like(mass)

        if it == 0:
            def largest(i, so_far):
                block = pts[pl.ds(pl.multiple_of(i * 128, 128), 128), :]
                return jnp.maximum(so_far, jnp.abs(block).reshape(8, 16, pts.shape[1]).max(axis=0))

            tile = lax.fori_loop(
                0, pts.shape[0] // 128, largest, jnp.zeros((16, pts.shape[1]), BF16)
            )
            size_bound = jnp.max(jnp.max(tile.astype(F32), axis=0, keepdims=True), axis=1, keepdims=True)

        def weigh(ch):
            all_stats(it, ch).wait_recv()
            every = stat[it, ch]
            row_max = jnp.max(every, axis=0)
            lse = row_max + jnp.log(jnp.sum(jnp.exp(every - row_max[None]), axis=0))
            if last:
                log_out[pl.ds(pl.multiple_of(ch * 8, 8), 8), :] = lse
            scale = jnp.exp(max_loc[ch] - lse)
            for half in range(2):
                cols = pl.ds(pl.multiple_of(ch * CHUNK + half * 512, 512), 512)
                row = jnp.concatenate([scale[j : j + 1, :] for j in range(half * 4, half * 4 + 4)], axis=1)
                weights = (expd[:, cols] * row).astype(BF16)
                wts[:, cols] = weights
                wide = weights.astype(F32)
                mass[...] += sum(wide[:, a : a + 128] for a in range(0, 512, 128))

        early = (n_chunks - 1) * CHUNK

        def slot(n):
            return at_y(offset_of(n)) if last else n

        def columns(n):
            return pl.ds(pl.multiple_of(slot(n) * COLS, COLS), COLS)

        def product(ch):
            cols = pl.ds(pl.multiple_of(ch * CHUNK, CHUNK), CHUNK)
            return jnp.dot(wts[:, cols], pts[cols, :], preferred_element_type=F32)

        weigh(0)
        first = product(0)
        if last:
            for n in range(n_cols):
                acc[n] = first[:, n * COLS : (n + 1) * COLS]
        else:
            acc_rows[...] = first

        @pl.loop(1, n_chunks - 1)
        def _(ch):
            weigh(ch)
            more = product(ch)
            if last:
                for n in range(n_cols):
                    acc[n] += more[:, n * COLS : (n + 1) * COLS]
            else:
                acc_rows[...] += more

        weigh(n_chunks - 1)

        for b in range(4):
            block = mass[b * 128 : (b + 1) * 128, :].T
            mass_all[it, p, 0:1, b * 128 : (b + 1) * 128] = jnp.sum(block, axis=0, keepdims=True)
        mass_all[it, p, 1:2, :] = jnp.broadcast_to(size_bound[0:1, 0:1], (1, mass_all.shape[3]))

        to_sib = lax.rem(8 + other - core, 8)
        mass_copy(it, to_sib, p, 0).start()

        @pl.loop(1, 8)
        def _(i):
            @pl.when(i != to_sib)
            def _():
                mass_copy(it, i, p, 1).start()

        def chip_mass(yy):
            row = mass_all[it, yy * 2, 0:1, :] + mass_all[it, yy * 2 + 1, 0:1, :]
            size = jnp.maximum(mass_all[it, yy * 2, 1:2, :], mass_all[it, yy * 2 + 1, 1:2, :])
            return row, jnp.maximum(row * size, 1e-30)

        def down(row, b):
            return jnp.broadcast_to(row[:, b * 128 : (b + 1) * 128], (128, 128)).T

        def finish_pair(n):
            sib_copy(it, n).wait_recv()
            if not last:
                pair[n] = acc_rows[half_rows(n, core), :] + sib_buf[n]
                for k in (2, 1, 3):
                    at = pl.multiple_of(at_y(k) * own_size, own_size)
                    scale = inverse[own_rows(n, at_y(k), core), :]
                    for h in range(pts.shape[1] // 128):
                        lanes = slice(h * 128, (h + 1) * 128)
                        row_code[n, k - 1, :, lanes] = encode(pair[n, pl.ds(at, own_size), lanes] * scale)
                    y_copy_rows(n, k).start()
            else:
                sums = acc[slot(n), :, pl.ds(pl.multiple_of(core * 128, 128), 128)] + col_buf[n]
                if isinstance(n, int):
                    return sums
                col_code[n] = encode(sums * inverse[...])
                y_copy_cols(n).start()

        def finish_sums(n):
            if last:
                acc[slot(n)] += jnp.dot(
                    wts[:, early:], pts[early:, columns(n)], preferred_element_type=F32
                )
            else:
                rows = pl.ds(pl.multiple_of(n * 2 * half_size, half_size), 2 * half_size)
                acc_rows[rows, :] += jnp.dot(wts[rows, early:], pts[early:, :], preferred_element_type=F32)
            sib_copy(it, n).start()

        finish_sums(0)
        all_masses(it, 1, 0).wait_recv()
        _, bound = chip_mass(y)
        for b in range(4):
            inverse[b * 128 : (b + 1) * 128, :] = down(1.0 / bound, b)

        @pl.loop(1, n_cols)
        def _(n):
            finish_sums(n)
            finish_pair(n - 1)

        own_sum = finish_pair(n_cols - 1)

        all_masses(it, 6, 1).wait_recv()

        total_mass, _ = chip_mass(y)
        for k in range(1, 4):
            row, bound = chip_mass(at_y(4 - k))
            total_mass = total_mass + row
            for b in range(4):
                bounds[k - 1, b * 128 : (b + 1) * 128, :] = down(bound, b)
        for b in range(4):
            mass_col[b * 128 : (b + 1) * 128, :] = jnp.maximum(down(total_mass, b), 1.0)

        if not last:
            @pl.loop(0, GROUPS)
            def _(g):
                all_rows(g).wait_recv()
                own = own_rows(g, y, core)
                at = pl.ds(pl.multiple_of(y * own_size, own_size), own_size)
                divisor = mass_col[own, :]
                squares = jnp.zeros((own_size, 128), F32)
                for h in range(pts.shape[1] // 128):
                    lanes = slice(h * 128, (h + 1) * 128)
                    v = pair[g, at, lanes]
                    for k in range(1, 4):
                        v = v + decode(row_got[g, k - 1, :, lanes]) * bounds[k - 1, own, :]
                    q = v / divisor
                    means_own[:, lanes] = q
                    squares = squares + q * q
                norm = lax.rsqrt(jnp.sum(squares, axis=1, keepdims=True) + 1e-06)
                unit[1, own, :] = (means_own[...] * norm).astype(BF16)
                for k in (2, 1, 3):
                    gather_y(g, k).start()

            sent(it)
            all_sent(y_send.at[0]).wait_send()

            @pl.loop(0, GROUPS)
            def _(g):
                all_gather_y(g).wait_recv()
                gather_sib(g).start()

            @pl.loop(0, GROUPS)
            def _(g):
                gather_sib(g).wait_recv()
        else:
            sent(it)
            all_sent(g_send.at[0]).wait_send()

            @pl.loop(0, GROUPS)
            def _(g):
                gather_sib(g).wait_send()

            result = own_sum
            for n, k in ((0, 2), (1, 1), (2, 3)):
                y_copy_cols(n).wait_recv()
                result = result + decode(col_got[n]) * bounds[k - 1]
            means_out[...] = result / mass_col[...]

    for n in range(3):
        y_copy_cols(n).wait_send()


def write_out(means, logs, means_out, log_out):
    means_out[...] = means[...]
    log_out[...] = logs[...]


def on_device(points, centroids):
    n_pts, depth = points.shape
    rows = centroids.shape[0]
    n_chunks, n_cols = n_pts // CHUNK, depth // COLS
    half, own = rows // (2 * GROUPS), rows // (8 * GROUPS)
    vmem, dma = pltpu.VMEM, pltpu.SemaphoreType.DMA
    means, logs = pl.pallas_call(
        kernel,
        out_shape=(
            jax.ShapeDtypeStruct((rows, 128), F32),
            jax.ShapeDtypeStruct((n_pts // 128, 128), F32),
        ),
        in_specs=[pl.BlockSpec(memory_space=pltpu.HBM)] * 2,
        out_specs=(pl.BlockSpec(memory_space=pltpu.VMEM),) * 2,
        scratch_shapes=[
            vmem((n_pts, depth), BF16),
            vmem((rows, depth), F32),
            vmem((2, rows, depth), BF16),
            vmem((rows, n_pts), F32),
            vmem((rows, n_pts), BF16),
            vmem((rows, 128), F32),
            vmem((n_chunks, 8, 128), F32),
            vmem((2, n_chunks, 16, 8, 128), F32),
            vmem((rows, depth), F32),
            vmem((n_cols, rows, COLS), F32),
            vmem((GROUPS, half, depth), F32),
            vmem((GROUPS, half, depth), F32),
            vmem((GROUPS, 3, own, depth), BF16),
            vmem((GROUPS, 3, own, depth), BF16),
            vmem((own, depth), F32),
            vmem((n_cols, rows, 128), F32),
            vmem((3, rows, 128), BF16),
            vmem((3, rows, 128), BF16),
            vmem((2, 8, 8, rows), F32),
            vmem((rows, 128), F32),
            vmem((3, rows, 128), F32),
            vmem((rows, 128), F32),
            dma((n_chunks + 4,)),
            dma((2, n_chunks)), dma((2, n_chunks)),
            dma((2, n_cols)), dma((2, n_cols)),
            dma((4,)), dma((2, 4)),
            dma((2,)), dma((2, 2)),
            dma((1,)), dma((GROUPS,)),
            dma((GROUPS,)), dma((GROUPS,)),
        ],
        compiler_params=pltpu.CompilerParams(
            collective_id=0, has_side_effects=True, vmem_limit_bytes=VMEM_LIMIT
        ),
        name="kmeans",
    )(points, centroids)
    means, logs = pl.pallas_call(
        write_out,
        out_shape=(
            jax.ShapeDtypeStruct(means.shape, F32), jax.ShapeDtypeStruct(logs.shape, F32),
        ),
        in_specs=[pl.BlockSpec(memory_space=pltpu.VMEM)] * 2,
        out_specs=(pl.BlockSpec(memory_space=pltpu.VMEM),) * 2,
        compiler_params=pltpu.CompilerParams(vmem_limit_bytes=4 * 1024 * 1024),
        name="write_out",
    )(means, logs)
    return means, logs.reshape(n_pts)


def solution(mesh):
    return jax.shard_map(
        on_device,
        mesh=mesh,
        in_specs=(P("pts", None), P("cen", None)),
        out_specs=(P("cen", "pts"), P("pts")),
        check_vma=False,
    )
```

```python
import functools
import jax
import jax.numpy as jnp
from jax import lax
from jax.experimental import pallas as pl
from jax.experimental.pallas import tpu as pltpu
from jax.sharding import PartitionSpec as P

ITERS = 2
VMEM_LIMIT = 52 * 1024 * 1024
MESH = pl.DeviceIdType.MESH
F32 = jnp.float32
BF16 = jnp.bfloat16
CHUNK = 1024
COLS = 256
FAR_FIRST = sorted(
    ((dx, dz) for dx in range(4) for dz in range(4) if dx or dz),
    key=lambda d: -min(d[0], 4 - d[0]) - min(d[1], 4 - d[1]),
)
GROUPS = 4


OCTAVES = 24.0
HALF = 117.0
STEPS = 2.0 * HALF / OCTAVES


def encode(ratio):
    u = jnp.maximum(jnp.log2(jnp.abs(ratio)) + OCTAVES, 0.0) * STEPS
    upper = jnp.floor(u)
    value = jnp.exp2(upper - HALF) * (1.0 + (u - upper))
    return jnp.where(ratio < 0.0, -value, value).astype(BF16)


def decode(code):
    value = code.astype(F32)
    size = jnp.abs(value)
    upper = jnp.floor(jnp.log2(size) + 0.004)
    u = upper + (HALF - 1.0) + size * jnp.exp2(-upper)
    ratio = jnp.exp2(u * (1.0 / STEPS) - OCTAVES)
    ratio = jnp.where(u < 0.004, 0.0, ratio)
    return jnp.where(value < 0.0, -ratio, ratio)


def kernel(
    pts_hbm, cen_hbm, means_out, log_out,
    pts, cen, unit, expd, wts, mass, max_loc, stat, acc_rows, acc, pair, sib_buf, row_code, row_got, means_own, col_buf,
    col_code, col_got, mass_all, inverse, bounds, mass_col,
    in_sem, st_send, st_recv, sib_send, sib_recv, y_send, y_recv, m_send, m_recv,
    g_send, g_recv, gs_send, gs_recv,
):
    p = lax.axis_index("pts")
    c = lax.axis_index("cen")
    y, core = p // 2, lax.rem(p, 2)
    other = 1 - core
    n_chunks = pts.shape[0] // CHUNK
    n_cols = pts.shape[1] // COLS
    half_size, own_size = pair.shape[1], pair.shape[1] // 4

    def cen_peer(dx, dz):
        return lax.rem(c // 4 + dx, 4) * 4 + lax.rem(lax.rem(c, 4) + dz, 4)

    def at_y(k):
        return lax.rem(y + k, 4)

    def y_peer(k):
        return (at_y(k) * 2 + core, c)

    sib_index = y * 2 + other
    sibling = (sib_index, c)

    def load_points(i):
        rows = pl.ds(pl.multiple_of(i * CHUNK, CHUNK), CHUNK)
        return pltpu.make_async_copy(pts_hbm.at[rows], pts.at[rows], in_sem.at[i])

    def load_cen(b):
        rows = pl.ds(pl.multiple_of(b * 128, 128), 128)
        return pltpu.make_async_copy(cen_hbm.at[rows], cen.at[rows], in_sem.at[n_chunks + b])

    @pl.loop(0, 4)
    def _(b):
        load_cen(b).start()

    @pl.loop(0, n_chunks)
    def _(i):
        load_points(i).start()

    barrier = pltpu.get_barrier_semaphore()

    for dx, dz in FAR_FIRST:
        pl.semaphore_signal(barrier, inc=1, device_id=(p, cen_peer(dx, dz)), device_id_type=MESH)
    pl.semaphore_signal(barrier, inc=1, device_id=sibling, device_id_type=MESH)
    for k in (2, 1, 3):
        for cc in (core, other):
            pl.semaphore_signal(barrier, inc=1, device_id=(at_y(k) * 2 + cc, c), device_id_type=MESH)

    @pl.loop(0, 4)
    def _(b):
        load_cen(b).wait()
        rows = pl.ds(pl.multiple_of(b * 128, 128), 128)
        v = cen[rows, :]
        squares = jnp.sum(v * v, axis=1, keepdims=True)
        unit[0, rows, :] = (v * lax.rsqrt(squares + 1e-06)).astype(BF16)

    def stat_copy(it, ch, peer):
        return pltpu.make_async_remote_copy(
            src_ref=stat.at[it, ch, c], dst_ref=stat.at[it, ch, c],
            send_sem=st_send.at[it, ch], recv_sem=st_recv.at[it, ch],
            device_id=(p, peer), device_id_type=MESH,
        )

    def offset_of(n):
        return lax.rem(jnp.where(n == 0, 2, jnp.where(n == 1, 1, jnp.where(n == 2, 3, 0))), 4)

    def all_stats(it, ch):
        some = stat.at[it, ch, pl.ds(0, 15)]
        return pltpu.make_async_remote_copy(
            src_ref=some, dst_ref=some, send_sem=st_send.at[it, ch], recv_sem=st_recv.at[it, ch],
            device_id=sibling, device_id_type=MESH,
        )

    def half_rows(g, cc):
        return pl.ds(pl.multiple_of(g * 2 * half_size + cc * half_size, half_size), half_size)

    def own_rows(g, yy, cc):
        return pl.ds(pl.multiple_of(g * 2 * half_size + cc * half_size + yy * own_size, own_size), own_size)

    def sib_copy(it, n):
        if it == 0:
            src, dst = acc_rows.at[half_rows(n, other)], sib_buf.at[n]
        else:
            src = acc.at[at_y(offset_of(n)), :, pl.ds(pl.multiple_of(other * 128, 128), 128)]
            dst = col_buf.at[n]
        return pltpu.make_async_remote_copy(
            src_ref=src, dst_ref=dst, send_sem=sib_send.at[it, n], recv_sem=sib_recv.at[it, n],
            device_id=sibling, device_id_type=MESH,
        )

    def y_copy_rows(n, k):
        return pltpu.make_async_remote_copy(
            src_ref=row_code.at[n, k - 1], dst_ref=row_got.at[n, k - 1],
            send_sem=y_send.at[0], recv_sem=y_recv.at[0, n],
            device_id=y_peer(k), device_id_type=MESH,
        )

    def y_copy_cols(n):
        k = offset_of(n)
        return pltpu.make_async_remote_copy(
            src_ref=col_code.at[n], dst_ref=col_got.at[n],
            send_sem=y_send.at[1 + n], recv_sem=y_recv.at[1, n],
            device_id=y_peer(k), device_id_type=MESH,
        )

    def all_masses(it, some, sem):
        some = mass_all.at[it, pl.ds(0, some)]
        return pltpu.make_async_remote_copy(
            src_ref=some, dst_ref=some, send_sem=m_send.at[it], recv_sem=m_recv.at[it, sem],
            device_id=sibling, device_id_type=MESH,
        )

    def mass_copy(it, peer, sem):
        return pltpu.make_async_remote_copy(
            src_ref=mass_all.at[it, p], dst_ref=mass_all.at[it, p],
            send_sem=m_send.at[it], recv_sem=m_recv.at[it, sem],
            device_id=(peer, c), device_id_type=MESH,
        )

    def all_rows(g):
        return pltpu.make_async_remote_copy(
            src_ref=row_code.at[g], dst_ref=row_got.at[g],
            send_sem=y_send.at[0], recv_sem=y_recv.at[0, g],
            device_id=sibling, device_id_type=MESH,
        )

    def all_sent(sem):
        return pltpu.make_async_remote_copy(
            src_ref=row_code, dst_ref=row_code, send_sem=sem, recv_sem=y_recv.at[0, 0],
            device_id=sibling, device_id_type=MESH,
        )

    def gather_y(g, k):
        rows = own_rows(g, y, core)
        return pltpu.make_async_remote_copy(
            src_ref=unit.at[1, rows], dst_ref=unit.at[1, rows],
            send_sem=g_send.at[0], recv_sem=g_recv.at[g],
            device_id=y_peer(k), device_id_type=MESH,
        )

    def all_gather_y(g):
        return pltpu.make_async_remote_copy(
            src_ref=row_code.at[g], dst_ref=row_got.at[g],
            send_sem=g_send.at[0], recv_sem=g_recv.at[g],
            device_id=sibling, device_id_type=MESH,
        )

    def gather_sib(g):
        rows = half_rows(g, core)
        return pltpu.make_async_remote_copy(
            src_ref=unit.at[1, rows], dst_ref=unit.at[1, rows],
            send_sem=gs_send.at[g], recv_sem=gs_recv.at[g],
            device_id=sibling, device_id_type=MESH,
        )

    def sent(it):
        @pl.loop(0, n_chunks)
        def _(ch):
            all_stats(it, ch).wait_send()

        all_masses(it, 7, 0).wait_send()

        @pl.loop(0, n_cols)
        def _(n):
            sib_copy(it, n).wait_send()

    for it in range(ITERS):
        last = it + 1 == ITERS

        @pl.loop(0, n_chunks)
        def _(ch):
            if it == 0:
                load_points(ch).wait()
            cols = pl.ds(pl.multiple_of(ch * CHUNK, CHUNK), CHUNK)
            logits = lax.dot_general(
                unit[it], pts[cols, :], (((1,), (1,)), ((), ())), preferred_element_type=F32
            )
            local_max = jnp.max(logits, axis=0, keepdims=True)
            shifted = jnp.exp(logits - local_max)
            total = jnp.sum(shifted, axis=0, keepdims=True)
            expd[:, cols] = shifted
            lse = local_max + jnp.log(total)
            for j in range(CHUNK // 128):
                max_loc[ch, j : j + 1, :] = local_max[:, j * 128 : (j + 1) * 128]
                stat[it, ch, c, j : j + 1, :] = lse[:, j * 128 : (j + 1) * 128]

            if it == 0:

                @pl.when(ch == 0)
                def _():
                    pl.semaphore_wait(barrier, 22)

            for dx, dz in FAR_FIRST:
                stat_copy(it, ch, cen_peer(dx, dz)).start()

        mass[...] = jnp.zeros_like(mass)

        if it == 0:
            def largest(i, so_far):
                block = pts[pl.ds(pl.multiple_of(i * 128, 128), 128), :]
                return jnp.maximum(so_far, jnp.abs(block).reshape(8, 16, pts.shape[1]).max(axis=0))

            tile = lax.fori_loop(
                0, pts.shape[0] // 128, largest, jnp.zeros((16, pts.shape[1]), BF16)
            )
            size_bound = jnp.max(jnp.max(tile.astype(F32), axis=0, keepdims=True), axis=1, keepdims=True)

        def weigh(ch):
            all_stats(it, ch).wait_recv()
            every = stat[it, ch]
            row_max = jnp.max(every, axis=0)
            lse = row_max + jnp.log(jnp.sum(jnp.exp(every - row_max[None]), axis=0))
            if last:
                log_out[pl.ds(pl.multiple_of(ch * 8, 8), 8), :] = lse
            scale = jnp.exp(max_loc[ch] - lse)
            for half in range(2):
                cols = pl.ds(pl.multiple_of(ch * CHUNK + half * 512, 512), 512)
                row = jnp.concatenate([scale[j : j + 1, :] for j in range(half * 4, half * 4 + 4)], axis=1)
                weights = (expd[:, cols] * row).astype(BF16)
                wts[:, cols] = weights
                wide = weights.astype(F32)
                mass[...] += sum(wide[:, a : a + 128] for a in range(0, 512, 128))

        early = (n_chunks - 1) * CHUNK

        def slot(n):
            return at_y(offset_of(n)) if last else n

        def columns(n):
            return pl.ds(pl.multiple_of(slot(n) * COLS, COLS), COLS)

        def product(ch):
            cols = pl.ds(pl.multiple_of(ch * CHUNK, CHUNK), CHUNK)
            return jnp.dot(wts[:, cols], pts[cols, :], preferred_element_type=F32)

        weigh(0)
        first = product(0)
        if last:
            for n in range(n_cols):
                acc[n] = first[:, n * COLS : (n + 1) * COLS]
        else:
            acc_rows[...] = first

        @pl.loop(1, n_chunks - 1)
        def _(ch):
            weigh(ch)
            more = product(ch)
            if last:
                for n in range(n_cols):
                    acc[n] += more[:, n * COLS : (n + 1) * COLS]
            else:
                acc_rows[...] += more

        weigh(n_chunks - 1)

        def finish_sums(n):
            if last:
                acc[slot(n)] += jnp.dot(
                    wts[:, early:], pts[early:, columns(n)], preferred_element_type=F32
                )
            else:
                rows = pl.ds(pl.multiple_of(n * 2 * half_size, half_size), 2 * half_size)
                acc_rows[rows, :] += jnp.dot(wts[rows, early:], pts[early:, :], preferred_element_type=F32)
            sib_copy(it, n).start()

        for b in range(4):
            block = mass[b * 128 : (b + 1) * 128, :].T
            mass_all[it, p, 0:1, b * 128 : (b + 1) * 128] = jnp.sum(block, axis=0, keepdims=True)
        mass_all[it, p, 1:2, :] = jnp.broadcast_to(size_bound[0:1, 0:1], (1, mass_all.shape[3]))

        mass_copy(it, sib_index, 0).start()
        for k in (2, 1, 3):
            for cc in (core, other):
                mass_copy(it, at_y(k) * 2 + cc, 1).start()

        finish_sums(0)

        def chip_mass(yy):
            row = mass_all[it, yy * 2, 0:1, :] + mass_all[it, yy * 2 + 1, 0:1, :]
            size = jnp.maximum(mass_all[it, yy * 2, 1:2, :], mass_all[it, yy * 2 + 1, 1:2, :])
            return row, jnp.maximum(row * size, 1e-30)

        def down(row, b):
            return jnp.broadcast_to(row[:, b * 128 : (b + 1) * 128], (128, 128)).T

        def finish_pair(n):
            sib_copy(it, n).wait_recv()
            if not last:
                pair[n] = acc_rows[half_rows(n, core), :] + sib_buf[n]
                for k in (2, 1, 3):
                    at = pl.multiple_of(at_y(k) * own_size, own_size)
                    scale = inverse[own_rows(n, at_y(k), core), :]
                    for h in range(pts.shape[1] // 128):
                        lanes = slice(h * 128, (h + 1) * 128)
                        row_code[n, k - 1, :, lanes] = encode(pair[n, pl.ds(at, own_size), lanes] * scale)
                    y_copy_rows(n, k).start()
            else:
                sums = acc[slot(n), :, pl.ds(pl.multiple_of(core * 128, 128), 128)] + col_buf[n]
                if isinstance(n, int):
                    return sums
                col_code[n] = encode(sums * inverse[...])
                y_copy_cols(n).start()

        all_masses(it, 1, 0).wait_recv()
        _, bound = chip_mass(y)
        for b in range(4):
            inverse[b * 128 : (b + 1) * 128, :] = down(1.0 / bound, b)

        @pl.loop(1, n_cols)
        def _(n):
            finish_sums(n)
            finish_pair(n - 1)

        own_sum = finish_pair(n_cols - 1)

        all_masses(it, 6, 1).wait_recv()

        total_mass, _ = chip_mass(y)
        for k in range(1, 4):
            row, bound = chip_mass(at_y(4 - k))
            total_mass = total_mass + row
            for b in range(4):
                bounds[k - 1, b * 128 : (b + 1) * 128, :] = down(bound, b)
        for b in range(4):
            mass_col[b * 128 : (b + 1) * 128, :] = jnp.maximum(down(total_mass, b), 1.0)

        if not last:
            @pl.loop(0, GROUPS)
            def _(g):
                all_rows(g).wait_recv()
                own = own_rows(g, y, core)
                at = pl.ds(pl.multiple_of(y * own_size, own_size), own_size)
                divisor = mass_col[own, :]
                squares = jnp.zeros((own_size, 128), F32)
                for h in range(pts.shape[1] // 128):
                    lanes = slice(h * 128, (h + 1) * 128)
                    v = pair[g, at, lanes]
                    for k in range(1, 4):
                        v = v + decode(row_got[g, k - 1, :, lanes]) * bounds[k - 1, own, :]
                    q = v / divisor
                    means_own[:, lanes] = q
                    squares = squares + q * q
                norm = lax.rsqrt(jnp.sum(squares, axis=1, keepdims=True) + 1e-06)
                unit[1, own, :] = (means_own[...] * norm).astype(BF16)
                for k in (2, 1, 3):
                    gather_y(g, k).start()

            sent(it)
            all_sent(y_send.at[0]).wait_send()

            @pl.loop(0, GROUPS)
            def _(g):
                all_gather_y(g).wait_recv()
                gather_sib(g).start()

            @pl.loop(0, GROUPS)
            def _(g):
                gather_sib(g).wait_recv()
        else:
            sent(it)
            all_sent(g_send.at[0]).wait_send()

            @pl.loop(0, GROUPS)
            def _(g):
                gather_sib(g).wait_send()

            result = own_sum
            for n, k in ((0, 2), (1, 1), (2, 3)):
                y_copy_cols(n).wait_recv()
                result = result + decode(col_got[n]) * bounds[k - 1]
            means_out[...] = result / mass_col[...]

    for n in range(3):
        y_copy_cols(n).wait_send()


def write_out(means, logs, means_out, log_out):
    means_out[...] = means[...]
    log_out[...] = logs[...]


def on_device(points, centroids):
    n_pts, depth = points.shape
    rows = centroids.shape[0]
    n_chunks, n_cols = n_pts // CHUNK, depth // COLS
    half, own = rows // (2 * GROUPS), rows // (8 * GROUPS)
    vmem, dma = pltpu.VMEM, pltpu.SemaphoreType.DMA
    means, logs = pl.pallas_call(
        kernel,
        out_shape=(
            jax.ShapeDtypeStruct((rows, 128), F32),
            jax.ShapeDtypeStruct((n_pts // 128, 128), F32),
        ),
        in_specs=[pl.BlockSpec(memory_space=pltpu.HBM)] * 2,
        out_specs=(pl.BlockSpec(memory_space=pltpu.VMEM),) * 2,
        scratch_shapes=[
            vmem((n_pts, depth), BF16),
            vmem((rows, depth), F32),
            vmem((2, rows, depth), BF16),
            vmem((rows, n_pts), F32),
            vmem((rows, n_pts), BF16),
            vmem((rows, 128), F32),
            vmem((n_chunks, 8, 128), F32),
            vmem((2, n_chunks, 16, 8, 128), F32),
            vmem((rows, depth), F32),
            vmem((n_cols, rows, COLS), F32),
            vmem((GROUPS, half, depth), F32),
            vmem((GROUPS, half, depth), F32),
            vmem((GROUPS, 3, own, depth), BF16),
            vmem((GROUPS, 3, own, depth), BF16),
            vmem((own, depth), F32),
            vmem((n_cols, rows, 128), F32),
            vmem((3, rows, 128), BF16),
            vmem((3, rows, 128), BF16),
            vmem((2, 8, 8, rows), F32),
            vmem((rows, 128), F32),
            vmem((3, rows, 128), F32),
            vmem((rows, 128), F32),
            dma((n_chunks + 4,)),
            dma((2, n_chunks)), dma((2, n_chunks)),
            dma((2, n_cols)), dma((2, n_cols)),
            dma((4,)), dma((2, 4)),
            dma((2,)), dma((2, 2)),
            dma((1,)), dma((GROUPS,)),
            dma((GROUPS,)), dma((GROUPS,)),
        ],
        compiler_params=pltpu.CompilerParams(
            collective_id=0, has_side_effects=True, vmem_limit_bytes=VMEM_LIMIT
        ),
        name="kmeans",
    )(points, centroids)
    means, logs = pl.pallas_call(
        write_out,
        out_shape=(
            jax.ShapeDtypeStruct(means.shape, F32), jax.ShapeDtypeStruct(logs.shape, F32),
        ),
        in_specs=[pl.BlockSpec(memory_space=pltpu.VMEM)] * 2,
        out_specs=(pl.BlockSpec(memory_space=pltpu.VMEM),) * 2,
        compiler_params=pltpu.CompilerParams(vmem_limit_bytes=4 * 1024 * 1024),
        name="write_out",
    )(means, logs)
    return means, logs.reshape(n_pts)


def solution(mesh):
    return jax.shard_map(
        on_device,
        mesh=mesh,
        in_specs=(P("pts", None), P("cen", None)),
        out_specs=(P("cen", "pts"), P("pts")),
        check_vma=False,
    )
```

```python
import functools
import jax
import jax.numpy as jnp
from jax import lax
from jax.experimental import pallas as pl
from jax.experimental.pallas import tpu as pltpu
from jax.sharding import PartitionSpec as P

ITERS = 2
VMEM_LIMIT = 52 * 1024 * 1024
MESH = pl.DeviceIdType.MESH
F32 = jnp.float32
BF16 = jnp.bfloat16
CHUNK = 1024
COLS = 256
FAR_FIRST = sorted(
    ((dx, dz) for dx in range(4) for dz in range(4) if dx or dz),
    key=lambda d: -min(d[0], 4 - d[0]) - min(d[1], 4 - d[1]),
)
GROUPS = 4


OCTAVES = 24.0
HALF = 117.0
STEPS = 2.0 * HALF / OCTAVES


def encode(ratio):
    u = jnp.maximum(jnp.log2(jnp.abs(ratio)) + OCTAVES, 0.0) * STEPS
    upper = jnp.floor(u)
    value = jnp.exp2(upper - HALF) * (1.0 + (u - upper))
    return jnp.where(ratio < 0.0, -value, value).astype(BF16)


def decode(code):
    value = code.astype(F32)
    size = jnp.abs(value)
    upper = jnp.floor(jnp.log2(size) + 0.004)
    u = upper + (HALF - 1.0) + size * jnp.exp2(-upper)
    ratio = jnp.exp2(u * (1.0 / STEPS) - OCTAVES)
    ratio = jnp.where(u < 0.004, 0.0, ratio)
    return jnp.where(value < 0.0, -ratio, ratio)


def kernel(
    pts_hbm, cen_hbm, means_out, log_out,
    pts, cen, unit, expd, wts, mass, max_loc, stat, acc_rows, acc, pair, sib_buf, row_code, row_got, means_own, col_buf,
    col_code, col_got, mass_all, inverse, bounds, mass_col, largest,
    in_sem, st_send, st_recv, sib_send, sib_recv, y_send, y_recv, m_send, m_recv,
    g_send, g_recv, gs_send, gs_recv,
):
    p = lax.axis_index("pts")
    c = lax.axis_index("cen")
    y, core = p // 2, lax.rem(p, 2)
    other = 1 - core
    n_chunks = pts.shape[0] // CHUNK
    n_cols = pts.shape[1] // COLS
    half_size, own_size = pair.shape[1], pair.shape[1] // 4

    def cen_peer(dx, dz):
        return lax.rem(c // 4 + dx, 4) * 4 + lax.rem(lax.rem(c, 4) + dz, 4)

    def at_y(k):
        return lax.rem(y + k, 4)

    def y_peer(k):
        return (at_y(k) * 2 + core, c)

    sib_index = y * 2 + other
    sibling = (sib_index, c)

    def load_points(i):
        rows = pl.ds(pl.multiple_of(i * CHUNK, CHUNK), CHUNK)
        return pltpu.make_async_copy(pts_hbm.at[rows], pts.at[rows], in_sem.at[i])

    def load_cen(b):
        rows = pl.ds(pl.multiple_of(b * 128, 128), 128)
        return pltpu.make_async_copy(cen_hbm.at[rows], cen.at[rows], in_sem.at[n_chunks + b])

    @pl.loop(0, 4)
    def _(b):
        load_cen(b).start()

    @pl.loop(0, n_chunks)
    def _(i):
        load_points(i).start()

    largest[...] = jnp.zeros_like(largest)
    barrier = pltpu.get_barrier_semaphore()

    for dx, dz in FAR_FIRST:
        pl.semaphore_signal(barrier, inc=1, device_id=(p, cen_peer(dx, dz)), device_id_type=MESH)
    pl.semaphore_signal(barrier, inc=1, device_id=sibling, device_id_type=MESH)
    for k in (2, 1, 3):
        for cc in (core, other):
            pl.semaphore_signal(barrier, inc=1, device_id=(at_y(k) * 2 + cc, c), device_id_type=MESH)

    @pl.loop(0, 4)
    def _(b):
        load_cen(b).wait()
        rows = pl.ds(pl.multiple_of(b * 128, 128), 128)
        v = cen[rows, :]
        squares = jnp.sum(v * v, axis=1, keepdims=True)
        unit[0, rows, :] = (v * lax.rsqrt(squares + 1e-06)).astype(BF16)

    def stat_copy(it, ch, peer):
        return pltpu.make_async_remote_copy(
            src_ref=stat.at[it, ch, c], dst_ref=stat.at[it, ch, c],
            send_sem=st_send.at[it, ch], recv_sem=st_recv.at[it, ch],
            device_id=(p, peer), device_id_type=MESH,
        )

    def offset_of(n):
        return lax.rem(jnp.where(n == 0, 2, jnp.where(n == 1, 1, jnp.where(n == 2, 3, 0))), 4)

    def all_stats(it, ch):
        some = stat.at[it, ch, pl.ds(0, 15)]
        return pltpu.make_async_remote_copy(
            src_ref=some, dst_ref=some, send_sem=st_send.at[it, ch], recv_sem=st_recv.at[it, ch],
            device_id=sibling, device_id_type=MESH,
        )

    def half_rows(g, cc):
        return pl.ds(pl.multiple_of(g * 2 * half_size + cc * half_size, half_size), half_size)

    def own_rows(g, yy, cc):
        return pl.ds(pl.multiple_of(g * 2 * half_size + cc * half_size + yy * own_size, own_size), own_size)

    def sib_copy(it, n):
        if it == 0:
            src, dst = acc_rows.at[half_rows(n, other)], sib_buf.at[n]
        else:
            src = acc.at[at_y(offset_of(n)), :, pl.ds(pl.multiple_of(other * 128, 128), 128)]
            dst = col_buf.at[n]
        return pltpu.make_async_remote_copy(
            src_ref=src, dst_ref=dst, send_sem=sib_send.at[it, n], recv_sem=sib_recv.at[it, n],
            device_id=sibling, device_id_type=MESH,
        )

    def y_copy_rows(n, k):
        return pltpu.make_async_remote_copy(
            src_ref=row_code.at[n, k - 1], dst_ref=row_got.at[n, k - 1],
            send_sem=y_send.at[0], recv_sem=y_recv.at[0, n],
            device_id=y_peer(k), device_id_type=MESH,
        )

    def y_copy_cols(n):
        k = offset_of(n)
        return pltpu.make_async_remote_copy(
            src_ref=col_code.at[n], dst_ref=col_got.at[n],
            send_sem=y_send.at[1 + n], recv_sem=y_recv.at[1, n],
            device_id=y_peer(k), device_id_type=MESH,
        )

    def all_masses(it, some, sem):
        some = mass_all.at[it, pl.ds(0, some)]
        return pltpu.make_async_remote_copy(
            src_ref=some, dst_ref=some, send_sem=m_send.at[it], recv_sem=m_recv.at[it, sem],
            device_id=sibling, device_id_type=MESH,
        )

    def mass_copy(it, peer, sem):
        return pltpu.make_async_remote_copy(
            src_ref=mass_all.at[it, p], dst_ref=mass_all.at[it, p],
            send_sem=m_send.at[it], recv_sem=m_recv.at[it, sem],
            device_id=(peer, c), device_id_type=MESH,
        )

    def all_rows(g):
        return pltpu.make_async_remote_copy(
            src_ref=row_code.at[g], dst_ref=row_got.at[g],
            send_sem=y_send.at[0], recv_sem=y_recv.at[0, g],
            device_id=sibling, device_id_type=MESH,
        )

    def all_sent(sem):
        return pltpu.make_async_remote_copy(
            src_ref=row_code, dst_ref=row_code, send_sem=sem, recv_sem=y_recv.at[0, 0],
            device_id=sibling, device_id_type=MESH,
        )

    def gather_y(g, k):
        rows = own_rows(g, y, core)
        return pltpu.make_async_remote_copy(
            src_ref=unit.at[1, rows], dst_ref=unit.at[1, rows],
            send_sem=g_send.at[0], recv_sem=g_recv.at[g],
            device_id=y_peer(k), device_id_type=MESH,
        )

    def all_gather_y(g):
        return pltpu.make_async_remote_copy(
            src_ref=row_code.at[g], dst_ref=row_got.at[g],
            send_sem=g_send.at[0], recv_sem=g_recv.at[g],
            device_id=sibling, device_id_type=MESH,
        )

    def gather_sib(g):
        rows = half_rows(g, core)
        return pltpu.make_async_remote_copy(
            src_ref=unit.at[1, rows], dst_ref=unit.at[1, rows],
            send_sem=gs_send.at[g], recv_sem=gs_recv.at[g],
            device_id=sibling, device_id_type=MESH,
        )

    def sent(it):
        @pl.loop(0, n_chunks)
        def _(ch):
            all_stats(it, ch).wait_send()

        all_masses(it, 7, 0).wait_send()

        @pl.loop(0, n_cols)
        def _(n):
            sib_copy(it, n).wait_send()

    for it in range(ITERS):
        last = it + 1 == ITERS

        @pl.loop(0, n_chunks)
        def _(ch):
            if it == 0:
                load_points(ch).wait()
            cols = pl.ds(pl.multiple_of(ch * CHUNK, CHUNK), CHUNK)
            logits = lax.dot_general(
                unit[it], pts[cols, :], (((1,), (1,)), ((), ())), preferred_element_type=F32
            )
            if it == 0:
                tiles = jnp.abs(pts[cols, :]).reshape(CHUNK // 16, 16, pts.shape[1])
                largest[...] = jnp.maximum(largest[...], jnp.max(tiles, axis=0))
            local_max = jnp.max(logits, axis=0, keepdims=True)
            shifted = jnp.exp(logits - local_max)
            total = jnp.sum(shifted, axis=0, keepdims=True)
            expd[:, cols] = shifted
            lse = local_max + jnp.log(total)
            for j in range(CHUNK // 128):
                max_loc[ch, j : j + 1, :] = local_max[:, j * 128 : (j + 1) * 128]
                stat[it, ch, c, j : j + 1, :] = lse[:, j * 128 : (j + 1) * 128]

            if it == 0:

                @pl.when(ch == 0)
                def _():
                    pl.semaphore_wait(barrier, 22)

            for dx, dz in FAR_FIRST:
                stat_copy(it, ch, cen_peer(dx, dz)).start()

        mass[...] = jnp.zeros_like(mass)

        if it == 0:
            size_bound = jnp.max(jnp.max(largest[...].astype(F32), axis=0, keepdims=True), axis=1, keepdims=True)

        def weigh(ch):
            all_stats(it, ch).wait_recv()
            every = stat[it, ch]
            row_max = jnp.max(every, axis=0)
            lse = row_max + jnp.log(jnp.sum(jnp.exp(every - row_max[None]), axis=0))
            if last:
                log_out[pl.ds(pl.multiple_of(ch * 8, 8), 8), :] = lse
            scale = jnp.exp(max_loc[ch] - lse)
            for half in range(2):
                cols = pl.ds(pl.multiple_of(ch * CHUNK + half * 512, 512), 512)
                row = jnp.concatenate([scale[j : j + 1, :] for j in range(half * 4, half * 4 + 4)], axis=1)
                weights = (expd[:, cols] * row).astype(BF16)
                wts[:, cols] = weights
                wide = weights.astype(F32)
                mass[...] += sum(wide[:, a : a + 128] for a in range(0, 512, 128))

        early = (n_chunks - 1) * CHUNK

        def slot(n):
            return at_y(offset_of(n)) if last else n

        def columns(n):
            return pl.ds(pl.multiple_of(slot(n) * COLS, COLS), COLS)

        def product(ch):
            cols = pl.ds(pl.multiple_of(ch * CHUNK, CHUNK), CHUNK)
            return jnp.dot(wts[:, cols], pts[cols, :], preferred_element_type=F32)

        weigh(0)
        first = product(0)
        if last:
            for n in range(n_cols):
                acc[n] = first[:, n * COLS : (n + 1) * COLS]
        else:
            acc_rows[...] = first

        @pl.loop(1, n_chunks - 1)
        def _(ch):
            weigh(ch)
            more = product(ch)
            if last:
                for n in range(n_cols):
                    acc[n] += more[:, n * COLS : (n + 1) * COLS]
            else:
                acc_rows[...] += more

        weigh(n_chunks - 1)

        def finish_sums(n):
            if last:
                acc[slot(n)] += jnp.dot(
                    wts[:, early:], pts[early:, columns(n)], preferred_element_type=F32
                )
            else:
                rows = pl.ds(pl.multiple_of(n * 2 * half_size, half_size), 2 * half_size)
                acc_rows[rows, :] += jnp.dot(wts[rows, early:], pts[early:, :], preferred_element_type=F32)
            sib_copy(it, n).start()

        for b in range(4):
            block = mass[b * 128 : (b + 1) * 128, :].T
            mass_all[it, p, 0:1, b * 128 : (b + 1) * 128] = jnp.sum(block, axis=0, keepdims=True)
        mass_all[it, p, 1:2, :] = jnp.broadcast_to(size_bound[0:1, 0:1], (1, mass_all.shape[3]))

        mass_copy(it, sib_index, 0).start()
        for k in (2, 1, 3):
            for cc in (core, other):
                mass_copy(it, at_y(k) * 2 + cc, 1).start()

        finish_sums(0)

        def chip_mass(yy):
            row = mass_all[it, yy * 2, 0:1, :] + mass_all[it, yy * 2 + 1, 0:1, :]
            size = jnp.maximum(mass_all[it, yy * 2, 1:2, :], mass_all[it, yy * 2 + 1, 1:2, :])
            return row, jnp.maximum(row * size, 1e-30)

        def down(row, b):
            return jnp.broadcast_to(row[:, b * 128 : (b + 1) * 128], (128, 128)).T

        def finish_pair(n):
            sib_copy(it, n).wait_recv()
            if not last:
                pair[n] = acc_rows[half_rows(n, core), :] + sib_buf[n]
                for k in (2, 1, 3):
                    at = pl.multiple_of(at_y(k) * own_size, own_size)
                    scale = inverse[own_rows(n, at_y(k), core), :]
                    for h in range(pts.shape[1] // 128):
                        lanes = slice(h * 128, (h + 1) * 128)
                        row_code[n, k - 1, :, lanes] = encode(pair[n, pl.ds(at, own_size), lanes] * scale)
                    y_copy_rows(n, k).start()
            else:
                sums = acc[slot(n), :, pl.ds(pl.multiple_of(core * 128, 128), 128)] + col_buf[n]
                if isinstance(n, int):
                    return sums
                col_code[n] = encode(sums * inverse[...])
                y_copy_cols(n).start()

        all_masses(it, 1, 0).wait_recv()
        _, bound = chip_mass(y)
        for b in range(4):
            inverse[b * 128 : (b + 1) * 128, :] = down(1.0 / bound, b)

        @pl.loop(1, n_cols)
        def _(n):
            finish_sums(n)
            finish_pair(n - 1)

        own_sum = finish_pair(n_cols - 1)

        all_masses(it, 6, 1).wait_recv()

        total_mass, _ = chip_mass(y)
        for k in range(1, 4):
            row, bound = chip_mass(at_y(4 - k))
            total_mass = total_mass + row
            for b in range(4):
                bounds[k - 1, b * 128 : (b + 1) * 128, :] = down(bound, b)
        for b in range(4):
            mass_col[b * 128 : (b + 1) * 128, :] = jnp.maximum(down(total_mass, b), 1.0)

        if not last:
            @pl.loop(0, GROUPS)
            def _(g):
                all_rows(g).wait_recv()
                own = own_rows(g, y, core)
                at = pl.ds(pl.multiple_of(y * own_size, own_size), own_size)
                divisor = mass_col[own, :]
                squares = jnp.zeros((own_size, 128), F32)
                for h in range(pts.shape[1] // 128):
                    lanes = slice(h * 128, (h + 1) * 128)
                    v = pair[g, at, lanes]
                    for k in range(1, 4):
                        v = v + decode(row_got[g, k - 1, :, lanes]) * bounds[k - 1, own, :]
                    q = v / divisor
                    means_own[:, lanes] = q
                    squares = squares + q * q
                norm = lax.rsqrt(jnp.sum(squares, axis=1, keepdims=True) + 1e-06)
                unit[1, own, :] = (means_own[...] * norm).astype(BF16)
                for k in (2, 1, 3):
                    gather_y(g, k).start()

            sent(it)
            all_sent(y_send.at[0]).wait_send()

            @pl.loop(0, GROUPS)
            def _(g):
                all_gather_y(g).wait_recv()
                gather_sib(g).start()

            @pl.loop(0, GROUPS)
            def _(g):
                gather_sib(g).wait_recv()
        else:
            sent(it)
            all_sent(g_send.at[0]).wait_send()

            @pl.loop(0, GROUPS)
            def _(g):
                gather_sib(g).wait_send()

            result = own_sum
            for n, k in ((0, 2), (1, 1), (2, 3)):
                y_copy_cols(n).wait_recv()
                result = result + decode(col_got[n]) * bounds[k - 1]
            means_out[...] = result / mass_col[...]

    for n in range(3):
        y_copy_cols(n).wait_send()


def write_out(means, logs, means_out, log_out):
    means_out[...] = means[...]
    log_out[...] = logs[...]


def on_device(points, centroids):
    n_pts, depth = points.shape
    rows = centroids.shape[0]
    n_chunks, n_cols = n_pts // CHUNK, depth // COLS
    half, own = rows // (2 * GROUPS), rows // (8 * GROUPS)
    vmem, dma = pltpu.VMEM, pltpu.SemaphoreType.DMA
    means, logs = pl.pallas_call(
        kernel,
        out_shape=(
            jax.ShapeDtypeStruct((rows, 128), F32),
            jax.ShapeDtypeStruct((n_pts // 128, 128), F32),
        ),
        in_specs=[pl.BlockSpec(memory_space=pltpu.HBM)] * 2,
        out_specs=(pl.BlockSpec(memory_space=pltpu.VMEM),) * 2,
        scratch_shapes=[
            vmem((n_pts, depth), BF16),
            vmem((rows, depth), F32),
            vmem((2, rows, depth), BF16),
            vmem((rows, n_pts), F32),
            vmem((rows, n_pts), BF16),
            vmem((rows, 128), F32),
            vmem((n_chunks, 8, 128), F32),
            vmem((2, n_chunks, 16, 8, 128), F32),
            vmem((rows, depth), F32),
            vmem((n_cols, rows, COLS), F32),
            vmem((GROUPS, half, depth), F32),
            vmem((GROUPS, half, depth), F32),
            vmem((GROUPS, 3, own, depth), BF16),
            vmem((GROUPS, 3, own, depth), BF16),
            vmem((own, depth), F32),
            vmem((n_cols, rows, 128), F32),
            vmem((3, rows, 128), BF16),
            vmem((3, rows, 128), BF16),
            vmem((2, 8, 8, rows), F32),
            vmem((rows, 128), F32),
            vmem((3, rows, 128), F32),
            vmem((rows, 128), F32),
            vmem((16, depth), BF16),
            dma((n_chunks + 4,)),
            dma((2, n_chunks)), dma((2, n_chunks)),
            dma((2, n_cols)), dma((2, n_cols)),
            dma((4,)), dma((2, 4)),
            dma((2,)), dma((2, 2)),
            dma((1,)), dma((GROUPS,)),
            dma((GROUPS,)), dma((GROUPS,)),
        ],
        compiler_params=pltpu.CompilerParams(
            collective_id=0, has_side_effects=True, vmem_limit_bytes=VMEM_LIMIT
        ),
        name="kmeans",
    )(points, centroids)
    means, logs = pl.pallas_call(
        write_out,
        out_shape=(
            jax.ShapeDtypeStruct(means.shape, F32), jax.ShapeDtypeStruct(logs.shape, F32),
        ),
        in_specs=[pl.BlockSpec(memory_space=pltpu.VMEM)] * 2,
        out_specs=(pl.BlockSpec(memory_space=pltpu.VMEM),) * 2,
        compiler_params=pltpu.CompilerParams(vmem_limit_bytes=4 * 1024 * 1024),
        name="write_out",
    )(means, logs)
    return means, logs.reshape(n_pts)


def solution(mesh):
    return jax.shard_map(
        on_device,
        mesh=mesh,
        in_specs=(P("pts", None), P("cen", None)),
        out_specs=(P("cen", "pts"), P("pts")),
        check_vma=False,
    )
```

```python
import functools
import jax
import jax.numpy as jnp
from jax import lax
from jax.experimental import pallas as pl
from jax.experimental.pallas import tpu as pltpu
from jax.sharding import PartitionSpec as P

ITERS = 2
VMEM_LIMIT = 52 * 1024 * 1024
MESH = pl.DeviceIdType.MESH
F32 = jnp.float32
BF16 = jnp.bfloat16
CHUNK = 1024
COLS = 256
FAR_FIRST = sorted(
    ((dx, dz) for dx in range(4) for dz in range(4) if dx or dz),
    key=lambda d: -min(d[0], 4 - d[0]) - min(d[1], 4 - d[1]),
)
GROUPS = 4


OCTAVES = 24.0
HALF = 117.0
STEPS = 2.0 * HALF / OCTAVES


def encode(ratio):
    u = jnp.maximum(jnp.log2(jnp.abs(ratio)) + OCTAVES, 0.0) * STEPS
    upper = jnp.floor(u)
    value = jnp.exp2(upper - HALF) * (1.0 + (u - upper))
    return jnp.where(ratio < 0.0, -value, value).astype(BF16)


def decode(code):
    value = code.astype(F32)
    size = jnp.abs(value)
    upper = jnp.floor(jnp.log2(size) + 0.004)
    u = upper + (HALF - 1.0) + size * jnp.exp2(-upper)
    ratio = jnp.exp2(u * (1.0 / STEPS) - OCTAVES)
    ratio = jnp.where(u < 0.004, 0.0, ratio)
    return jnp.where(value < 0.0, -ratio, ratio)


def kernel(
    pts_hbm, cen_hbm, means_out, log_out,
    pts, cen, unit, expd, wts, mass, max_loc, stat, acc_rows, acc, pair, sib_buf, row_code, row_got, means_own, col_buf,
    col_code, col_got, mass_all, inverse, bounds, mass_col, largest,
    in_sem, st_send, st_recv, sib_send, sib_recv, y_send, y_recv, m_send, m_recv,
    g_send, g_recv, gs_send, gs_recv,
):
    p = lax.axis_index("pts")
    c = lax.axis_index("cen")
    y, core = p // 2, lax.rem(p, 2)
    other = 1 - core
    n_chunks = pts.shape[0] // CHUNK
    n_cols = pts.shape[1] // COLS
    half_size, own_size = pair.shape[1], pair.shape[1] // 4

    def cen_peer(dx, dz):
        return lax.rem(c // 4 + dx, 4) * 4 + lax.rem(lax.rem(c, 4) + dz, 4)

    def at_y(k):
        return lax.rem(y + k, 4)

    def y_peer(k):
        return (at_y(k) * 2 + core, c)

    sib_index = y * 2 + other
    sibling = (sib_index, c)

    def load_points(i):
        rows = pl.ds(pl.multiple_of(i * CHUNK, CHUNK), CHUNK)
        return pltpu.make_async_copy(pts_hbm.at[rows], pts.at[rows], in_sem.at[i])

    def load_cen(b):
        rows = pl.ds(pl.multiple_of(b * 128, 128), 128)
        return pltpu.make_async_copy(cen_hbm.at[rows], cen.at[rows], in_sem.at[n_chunks + b])

    @pl.loop(0, 4)
    def _(b):
        load_cen(b).start()

    @pl.loop(0, n_chunks)
    def _(i):
        load_points(i).start()

    largest[...] = jnp.zeros_like(largest)
    barrier = pltpu.get_barrier_semaphore()

    for dx, dz in FAR_FIRST:
        pl.semaphore_signal(barrier, inc=1, device_id=(p, cen_peer(dx, dz)), device_id_type=MESH)
    pl.semaphore_signal(barrier, inc=1, device_id=sibling, device_id_type=MESH)
    for k in (2, 1, 3):
        for cc in (core, other):
            pl.semaphore_signal(barrier, inc=1, device_id=(at_y(k) * 2 + cc, c), device_id_type=MESH)

    @pl.loop(0, 4)
    def _(b):
        load_cen(b).wait()
        rows = pl.ds(pl.multiple_of(b * 128, 128), 128)
        v = cen[rows, :]
        squares = jnp.sum(v * v, axis=1, keepdims=True)
        unit[0, rows, :] = (v * lax.rsqrt(squares + 1e-06)).astype(BF16)

    def stat_copy(it, ch, peer):
        return pltpu.make_async_remote_copy(
            src_ref=stat.at[it, ch, c], dst_ref=stat.at[it, ch, c],
            send_sem=st_send.at[it, ch], recv_sem=st_recv.at[it, ch],
            device_id=(p, peer), device_id_type=MESH,
        )

    def offset_of(n):
        return lax.rem(jnp.where(n == 0, 2, jnp.where(n == 1, 1, jnp.where(n == 2, 3, 0))), 4)

    def all_stats(it, ch):
        some = stat.at[it, ch, pl.ds(0, 15)]
        return pltpu.make_async_remote_copy(
            src_ref=some, dst_ref=some, send_sem=st_send.at[it, ch], recv_sem=st_recv.at[it, ch],
            device_id=sibling, device_id_type=MESH,
        )

    def half_rows(g, cc):
        return pl.ds(pl.multiple_of(g * 2 * half_size + cc * half_size, half_size), half_size)

    def own_rows(g, yy, cc):
        return pl.ds(pl.multiple_of(g * 2 * half_size + cc * half_size + yy * own_size, own_size), own_size)

    def sib_copy(it, n):
        if it == 0:
            src, dst = acc_rows.at[half_rows(n, other)], sib_buf.at[n]
        else:
            src = acc.at[at_y(offset_of(n)), :, pl.ds(pl.multiple_of(other * 128, 128), 128)]
            dst = col_buf.at[n]
        return pltpu.make_async_remote_copy(
            src_ref=src, dst_ref=dst, send_sem=sib_send.at[it, n], recv_sem=sib_recv.at[it, n],
            device_id=sibling, device_id_type=MESH,
        )

    def y_copy_rows(n, k):
        return pltpu.make_async_remote_copy(
            src_ref=row_code.at[n, k - 1], dst_ref=row_got.at[n, k - 1],
            send_sem=y_send.at[0], recv_sem=y_recv.at[0, n],
            device_id=y_peer(k), device_id_type=MESH,
        )

    def y_copy_cols(n):
        k = offset_of(n)
        return pltpu.make_async_remote_copy(
            src_ref=col_code.at[n], dst_ref=col_got.at[n],
            send_sem=y_send.at[1 + n], recv_sem=y_recv.at[1, n],
            device_id=y_peer(k), device_id_type=MESH,
        )

    def all_masses(it, some, sem):
        some = mass_all.at[it, pl.ds(0, some)]
        return pltpu.make_async_remote_copy(
            src_ref=some, dst_ref=some, send_sem=m_send.at[it], recv_sem=m_recv.at[it, sem],
            device_id=sibling, device_id_type=MESH,
        )

    def mass_copy(it, peer, sem):
        return pltpu.make_async_remote_copy(
            src_ref=mass_all.at[it, p], dst_ref=mass_all.at[it, p],
            send_sem=m_send.at[it], recv_sem=m_recv.at[it, sem],
            device_id=(peer, c), device_id_type=MESH,
        )

    def all_rows(g):
        return pltpu.make_async_remote_copy(
            src_ref=row_code.at[g], dst_ref=row_got.at[g],
            send_sem=y_send.at[0], recv_sem=y_recv.at[0, g],
            device_id=sibling, device_id_type=MESH,
        )

    def all_sent(sem):
        return pltpu.make_async_remote_copy(
            src_ref=row_code, dst_ref=row_code, send_sem=sem, recv_sem=y_recv.at[0, 0],
            device_id=sibling, device_id_type=MESH,
        )

    def gather_y(g, k):
        rows = own_rows(g, y, core)
        return pltpu.make_async_remote_copy(
            src_ref=unit.at[1, rows], dst_ref=unit.at[1, rows],
            send_sem=g_send.at[0], recv_sem=g_recv.at[g],
            device_id=y_peer(k), device_id_type=MESH,
        )

    def all_gather_y(g):
        return pltpu.make_async_remote_copy(
            src_ref=row_code.at[g], dst_ref=row_got.at[g],
            send_sem=g_send.at[0], recv_sem=g_recv.at[g],
            device_id=sibling, device_id_type=MESH,
        )

    def gather_sib(g):
        rows = half_rows(g, core)
        return pltpu.make_async_remote_copy(
            src_ref=unit.at[1, rows], dst_ref=unit.at[1, rows],
            send_sem=gs_send.at[g], recv_sem=gs_recv.at[g],
            device_id=sibling, device_id_type=MESH,
        )

    def sent(it):
        @pl.loop(0, n_chunks)
        def _(ch):
            all_stats(it, ch).wait_send()

        all_masses(it, 7, 0).wait_send()

        @pl.loop(0, n_cols)
        def _(n):
            sib_copy(it, n).wait_send()

    for it in range(ITERS):
        last = it + 1 == ITERS

        @pl.loop(0, n_chunks)
        def _(ch):
            if it == 0:
                load_points(ch).wait()
            cols = pl.ds(pl.multiple_of(ch * CHUNK, CHUNK), CHUNK)
            logits = lax.dot_general(
                unit[it], pts[cols, :], (((1,), (1,)), ((), ())), preferred_element_type=F32
            )
            if it == 0:
                tiles = jnp.abs(pts[cols, :]).reshape(CHUNK // 16, 16, pts.shape[1])
                largest[...] = jnp.maximum(largest[...], jnp.max(tiles, axis=0))
            local_max = jnp.max(logits, axis=0, keepdims=True)
            shifted = jnp.exp(logits - local_max)
            total = jnp.sum(shifted, axis=0, keepdims=True)
            expd[:, cols] = shifted
            lse = local_max + jnp.log(total)
            for j in range(CHUNK // 128):
                max_loc[ch, j : j + 1, :] = local_max[:, j * 128 : (j + 1) * 128]
                stat[it, ch, c, j : j + 1, :] = lse[:, j * 128 : (j + 1) * 128]

            if it == 0:

                @pl.when(ch == 0)
                def _():
                    pl.semaphore_wait(barrier, 22)

            for dx, dz in FAR_FIRST:
                stat_copy(it, ch, cen_peer(dx, dz)).start()

        mass[...] = jnp.zeros_like(mass)

        if it == 0:
            size_bound = jnp.max(jnp.max(largest[...].astype(F32), axis=0, keepdims=True), axis=1, keepdims=True)

        def weigh(ch):
            all_stats(it, ch).wait_recv()
            every = stat[it, ch]
            row_max = jnp.max(every, axis=0)
            lse = row_max + jnp.log(jnp.sum(jnp.exp(every - row_max[None]), axis=0))
            if last:
                log_out[pl.ds(pl.multiple_of(ch * 8, 8), 8), :] = lse
            scale = jnp.exp(max_loc[ch] - lse)
            for half in range(2):
                cols = pl.ds(pl.multiple_of(ch * CHUNK + half * 512, 512), 512)
                row = jnp.concatenate([scale[j : j + 1, :] for j in range(half * 4, half * 4 + 4)], axis=1)
                weights = (expd[:, cols] * row).astype(BF16)
                wts[:, cols] = weights
                wide = weights.astype(F32)
                mass[...] += sum(wide[:, a : a + 128] for a in range(0, 512, 128))

        early = (n_chunks - 1) * CHUNK

        def slot(n):
            return at_y(offset_of(n)) if last else n

        def columns(n):
            return pl.ds(pl.multiple_of(slot(n) * COLS, COLS), COLS)

        def product(ch):
            cols = pl.ds(pl.multiple_of(ch * CHUNK, CHUNK), CHUNK)
            return jnp.dot(wts[:, cols], pts[cols, :], preferred_element_type=F32)

        weigh(0)
        first = product(0)
        if last:
            for n in range(n_cols):
                acc[n] = first[:, n * COLS : (n + 1) * COLS]
        else:
            acc_rows[...] = first

        @pl.loop(1, n_chunks - 1)
        def _(ch):
            weigh(ch)
            more = product(ch)
            if last:
                for n in range(n_cols):
                    acc[n] += more[:, n * COLS : (n + 1) * COLS]
            else:
                acc_rows[...] += more

        weigh(n_chunks - 1)

        def finish_sums(n):
            if last:
                acc[slot(n)] += jnp.dot(
                    wts[:, early:], pts[early:, columns(n)], preferred_element_type=F32
                )
            else:
                rows = pl.ds(pl.multiple_of(n * 2 * half_size, half_size), 2 * half_size)
                acc_rows[rows, :] += jnp.dot(wts[rows, early:], pts[early:, :], preferred_element_type=F32)
            sib_copy(it, n).start()

        for b in range(4):
            block = mass[b * 128 : (b + 1) * 128, :].T
            mass_all[it, p, 0:1, b * 128 : (b + 1) * 128] = jnp.sum(block, axis=0, keepdims=True)
        mass_all[it, p, 1:2, :] = jnp.broadcast_to(size_bound[0:1, 0:1], (1, mass_all.shape[3]))

        mass_copy(it, sib_index, 0).start()
        for k in (2, 1, 3):
            for cc in (core, other):
                mass_copy(it, at_y(k) * 2 + cc, 1).start()

        finish_sums(0)

        def chip_mass(yy):
            row = mass_all[it, yy * 2, 0:1, :] + mass_all[it, yy * 2 + 1, 0:1, :]
            size = jnp.maximum(mass_all[it, yy * 2, 1:2, :], mass_all[it, yy * 2 + 1, 1:2, :])
            return row, jnp.maximum(row * size, 1e-30)

        def down(row, b):
            return jnp.broadcast_to(row[:, b * 128 : (b + 1) * 128], (128, 128)).T

        def finish_pair(n):
            sib_copy(it, n).wait_recv()
            if not last:
                pair[n] = acc_rows[half_rows(n, core), :] + sib_buf[n]
                for k in (2, 1, 3):
                    at = pl.multiple_of(at_y(k) * own_size, own_size)
                    scale = inverse[own_rows(n, at_y(k), core), :]
                    for h in range(pts.shape[1] // 128):
                        lanes = slice(h * 128, (h + 1) * 128)
                        row_code[n, k - 1, :, lanes] = encode(pair[n, pl.ds(at, own_size), lanes] * scale)
                    y_copy_rows(n, k).start()
            else:
                sums = acc[slot(n), :, pl.ds(pl.multiple_of(core * 128, 128), 128)] + col_buf[n]
                if isinstance(n, int):
                    return sums
                col_code[n] = encode(sums * inverse[...])
                y_copy_cols(n).start()

        all_masses(it, 1, 0).wait_recv()
        _, bound = chip_mass(y)
        for b in range(4):
            inverse[b * 128 : (b + 1) * 128, :] = down(1.0 / bound, b)

        @pl.loop(1, n_cols)
        def _(n):
            finish_sums(n)
            finish_pair(n - 1)

        own_sum = finish_pair(n_cols - 1)

        all_masses(it, 6, 1).wait_recv()

        total_mass, _ = chip_mass(y)
        for k in range(1, 4):
            row, bound = chip_mass(at_y(4 - k))
            total_mass = total_mass + row
            for b in range(4):
                bounds[k - 1, b * 128 : (b + 1) * 128, :] = down(bound, b)
        for b in range(4):
            mass_col[b * 128 : (b + 1) * 128, :] = down(1.0 / jnp.maximum(total_mass, 1.0), b)

        if not last:
            @pl.loop(0, GROUPS)
            def _(g):
                all_rows(g).wait_recv()
                own = own_rows(g, y, core)
                at = pl.ds(pl.multiple_of(y * own_size, own_size), own_size)
                divisor = mass_col[own, :]
                squares = jnp.zeros((own_size, 128), F32)
                for h in range(pts.shape[1] // 128):
                    lanes = slice(h * 128, (h + 1) * 128)
                    v = pair[g, at, lanes]
                    for k in range(1, 4):
                        v = v + decode(row_got[g, k - 1, :, lanes]) * bounds[k - 1, own, :]
                    q = v * divisor
                    means_own[:, lanes] = q
                    squares = squares + q * q
                norm = lax.rsqrt(jnp.sum(squares, axis=1, keepdims=True) + 1e-06)
                unit[1, own, :] = (means_own[...] * norm).astype(BF16)
                for k in (2, 1, 3):
                    gather_y(g, k).start()

            sent(it)
            all_sent(y_send.at[0]).wait_send()

            @pl.loop(0, GROUPS)
            def _(g):
                all_gather_y(g).wait_recv()
                gather_sib(g).start()

            @pl.loop(0, GROUPS)
            def _(g):
                gather_sib(g).wait_recv()
        else:
            sent(it)
            all_sent(g_send.at[0]).wait_send()

            @pl.loop(0, GROUPS)
            def _(g):
                gather_sib(g).wait_send()

            result = own_sum
            for n, k in ((0, 2), (1, 1), (2, 3)):
                y_copy_cols(n).wait_recv()
                result = result + decode(col_got[n]) * bounds[k - 1]
            means_out[...] = result * mass_col[...]

    for n in range(3):
        y_copy_cols(n).wait_send()


def write_out(means, logs, means_out, log_out):
    means_out[...] = means[...]
    log_out[...] = logs[...]


def on_device(points, centroids):
    n_pts, depth = points.shape
    rows = centroids.shape[0]
    n_chunks, n_cols = n_pts // CHUNK, depth // COLS
    half, own = rows // (2 * GROUPS), rows // (8 * GROUPS)
    vmem, dma = pltpu.VMEM, pltpu.SemaphoreType.DMA
    means, logs = pl.pallas_call(
        kernel,
        out_shape=(
            jax.ShapeDtypeStruct((rows, 128), F32),
            jax.ShapeDtypeStruct((n_pts // 128, 128), F32),
        ),
        in_specs=[pl.BlockSpec(memory_space=pltpu.HBM)] * 2,
        out_specs=(pl.BlockSpec(memory_space=pltpu.VMEM),) * 2,
        scratch_shapes=[
            vmem((n_pts, depth), BF16),
            vmem((rows, depth), F32),
            vmem((2, rows, depth), BF16),
            vmem((rows, n_pts), F32),
            vmem((rows, n_pts), BF16),
            vmem((rows, 128), F32),
            vmem((n_chunks, 8, 128), F32),
            vmem((2, n_chunks, 16, 8, 128), F32),
            vmem((rows, depth), F32),
            vmem((n_cols, rows, COLS), F32),
            vmem((GROUPS, half, depth), F32),
            vmem((GROUPS, half, depth), F32),
            vmem((GROUPS, 3, own, depth), BF16),
            vmem((GROUPS, 3, own, depth), BF16),
            vmem((own, depth), F32),
            vmem((n_cols, rows, 128), F32),
            vmem((3, rows, 128), BF16),
            vmem((3, rows, 128), BF16),
            vmem((2, 8, 8, rows), F32),
            vmem((rows, 128), F32),
            vmem((3, rows, 128), F32),
            vmem((rows, 128), F32),
            vmem((16, depth), BF16),
            dma((n_chunks + 4,)),
            dma((2, n_chunks)), dma((2, n_chunks)),
            dma((2, n_cols)), dma((2, n_cols)),
            dma((4,)), dma((2, 4)),
            dma((2,)), dma((2, 2)),
            dma((1,)), dma((GROUPS,)),
            dma((GROUPS,)), dma((GROUPS,)),
        ],
        compiler_params=pltpu.CompilerParams(
            collective_id=0, has_side_effects=True, vmem_limit_bytes=VMEM_LIMIT
        ),
        name="kmeans",
    )(points, centroids)
    means, logs = pl.pallas_call(
        write_out,
        out_shape=(
            jax.ShapeDtypeStruct(means.shape, F32), jax.ShapeDtypeStruct(logs.shape, F32),
        ),
        in_specs=[pl.BlockSpec(memory_space=pltpu.VMEM)] * 2,
        out_specs=(pl.BlockSpec(memory_space=pltpu.VMEM),) * 2,
        compiler_params=pltpu.CompilerParams(vmem_limit_bytes=4 * 1024 * 1024),
        name="write_out",
    )(means, logs)
    return means, logs.reshape(n_pts)


def solution(mesh):
    return jax.shard_map(
        on_device,
        mesh=mesh,
        in_specs=(P("pts", None), P("cen", None)),
        out_specs=(P("cen", "pts"), P("pts")),
        check_vma=False,
    )
```
